128 devices in a mesh: dom: 32 (over z, y, core), feat: 4 (over x).
Axes of the slice: x: 4, y: 4, z: 4, core: 2. Of those that a mesh axis runs over, the one named last changes fastest.
Arguments:
- features: bfloat16 [128, 131072], P('feat', 'dom'), may hold values from -6 to 6
- edge_source: int32 [32, 32, 512], P('dom'), may hold values from 0 to 4095
- edge_target: int32 [32, 32, 512], P(None, 'dom'), may hold values from 0 to 4095
- edge_count: int32 [32, 32], P(None, 'dom'), may hold values from 128 to 512, as said below
- hub_local: int32 [32, 64], P('dom'), may hold values from 0 to 4095, as said below
- second_source: int32 [32768, 10], P('dom'), may hold values from 0 to 6143
- self_one: bfloat16 [128, 256], replicated, may hold values from -0.5 to 0.5
- neigh_one: bfloat16 [128, 256], replicated, may hold values from -0.5 to 0.5
- self_two: bfloat16 [256, 256], replicated, may hold values from -0.375 to 0.375
- neigh_two: bfloat16 [256, 256], replicated, may hold values from -0.375 to 0.375
Outputs:
- embedding: bfloat16 [256, 32768], P('feat', 'dom')
The draws below stay inside these ranges and needn't reach their ends.
Inputs may be any that keep to these rules, and one draw needn't show every extreme that they name: `edge_count`: one owner gets 512 live slots from every sender, and every sender fills 512 slots to some owner. `hub_local`: the ids of one owner's row are distinct.
All inputs are finite; a program needn't handle non-finite values.
Results may differ from the reference program's by a relative error of at most 0.0052.
Values may be sent and summed in bfloat16 or wider, within the bound.
A program may use at most 64 MiB of HBM per device.

```python
import jax
import jax.numpy as jnp

F = 128
H = 256
NODE_DEV = 4096
TGT_DEV = 1024
HUB_DEV = 64
FAN = 10
SLOTS = 512
NODES = 131072
TARGETS = 32768
HUBS = 2048
N_DOM = 32


def draw_edge_count(key, part):
    first, second, third = jax.random.split(jax.random.fold_in(key, 11), 3)
    counts = jax.random.randint(first, (N_DOM, N_DOM), SLOTS // 4, SLOTS + 1)
    picked = jax.random.randint(second, (N_DOM, 1), 0, N_DOM)
    column = jax.random.randint(third, (), 0, N_DOM)
    index = jnp.arange(N_DOM)[None, :]
    counts = jnp.where((index == picked) | (index == column), SLOTS, counts)
    return counts.astype(jnp.int32)


def draw_hub_local(key, part):
    keys = jax.random.split(jax.random.fold_in(key, 23), N_DOM)
    rows = jax.vmap(lambda k: jax.random.permutation(k, NODE_DEV)[:HUB_DEV])(keys)
    return rows.astype(jnp.int32)


def draw_second_source(key, part):
    first, second, third = jax.random.split(jax.random.fold_in(key, 37), 3)
    coin = jax.random.randint(first, (TARGETS, FAN), 0, 2)
    local_ids = jax.random.randint(second, (TARGETS, FAN), 0, NODE_DEV)
    hub_ids = NODE_DEV + jax.random.randint(third, (TARGETS, FAN), 0, HUBS)
    values = jnp.where(coin == 1, hub_ids, local_ids)
    values = values.at[0, 0].set(NODE_DEV + HUBS - 1)
    values = values.at[0, 1].set(0)
    return values.astype(jnp.int32)


def plant(result, key, smallest, top_value):
    extent = result.shape
    place = [jax.random.randint(jax.random.fold_in(key, axis), (), 0, extent[axis]) for axis in range(len(extent))]
    result = result.at[tuple(place)].set(smallest)
    longest = extent.index(max(extent))
    place[longest] = (place[longest] + 1) % extent[longest]
    return result.at[tuple(place)].set(top_value)


def steps_of(rng, shape, shards, low, high):
    def one(position, parts):
        steps = jax.random.uniform(jax.random.fold_in(jax.random.fold_in(rng, 6), position), (parts,), jnp.float32, low / len(shards), high / len(shards))
        return jnp.repeat(jnp.exp(steps), shape[position] // parts).reshape((-1,) + (1,) * (len(shape) - position - 1))

    gain = one(*shards[0])
    for cut in shards[1:]:
        gain = gain * one(*cut)
    return gain


def scatter_about(stream_key, extent, width, limit, cuts=(), kind=jnp.bfloat16):
    level = steps_of(stream_key, extent, cuts, -0.22, 0.18) if cuts else 1.0
    entries = jax.random.normal(stream_key, extent, jnp.float32) * width * level
    return jnp.minimum(jnp.maximum(entries, -limit), limit).astype(kind)


def setup_inputs(seed: int = 0) -> dict:
    arg_keys = jax.random.split(jax.random.key(seed), 11)
    return {
        "features": scatter_about(arg_keys[0], (F, NODES), 1.0, 6.0, ((0, 4), (1, 32))),
        "edge_source": plant(jax.random.randint(arg_keys[1], (N_DOM, N_DOM, SLOTS), 0, NODE_DEV), jax.random.fold_in(arg_keys[1], 1), 0, NODE_DEV - 1).astype(jnp.int32),
        "edge_target": plant(jax.random.randint(arg_keys[2], (N_DOM, N_DOM, SLOTS), 0, NODE_DEV), jax.random.fold_in(arg_keys[2], 1), 0, NODE_DEV - 1).astype(jnp.int32),
        "edge_count": draw_edge_count(jax.random.fold_in(arg_keys[10], 71), 0),
        "hub_local": draw_hub_local(jax.random.fold_in(arg_keys[10], 71), 0),
        "second_source": draw_second_source(jax.random.fold_in(arg_keys[10], 71), 0),
        "self_one": scatter_about(arg_keys[6], (F, H), F ** -0.5, 0.5),
        "neigh_one": scatter_about(arg_keys[7], (F, H), F ** -0.5, 0.5),
        "self_two": scatter_about(arg_keys[8], (H, H), H ** -0.5, 0.375),
        "neigh_two": scatter_about(arg_keys[9], (H, H), H ** -0.5, 0.375),
    }


def reference(features, edge_source, edge_target, edge_count, hub_local, second_source, self_one, neigh_one, self_two, neigh_two):
    node_rows = features.T
    sender = jnp.arange(N_DOM, dtype=jnp.int32)[:, None, None]
    owner = jnp.arange(N_DOM, dtype=jnp.int32)[None, :, None]
    slot = jnp.arange(SLOTS, dtype=jnp.int32)[None, None, :]
    live = (slot < edge_count[:, :, None]).reshape(-1)
    global_src = (sender * NODE_DEV + edge_source).reshape(-1)
    global_dst = (owner * NODE_DEV + edge_target).reshape(-1)
    live_f = live.astype(jnp.float32)
    degree = jax.ops.segment_sum(live_f, global_dst, num_segments=NODES)
    rows = node_rows[global_src].astype(jnp.float32) * live_f[:, None]
    sums = jax.ops.segment_sum(rows, global_dst, num_segments=NODES)
    mean_one = (sums / jnp.maximum(degree, 1.0)[:, None]).astype(jnp.bfloat16)
    pre = jnp.dot(node_rows, self_one, preferred_element_type=jnp.float32) + jnp.dot(mean_one, neigh_one, preferred_element_type=jnp.float32)
    hidden_one = jnp.maximum(pre, 0.0).astype(jnp.bfloat16)
    hub_index = (jnp.arange(N_DOM, dtype=jnp.int32)[:, None] * NODE_DEV + hub_local).reshape(-1)
    hub_rows = hidden_one[hub_index]
    table = jnp.concatenate([hidden_one, hub_rows], axis=0)
    part = (jnp.arange(TARGETS, dtype=jnp.int32) // TGT_DEV)[:, None]
    index = jnp.where(second_source < NODE_DEV, part * NODE_DEV + second_source, NODES + second_source - NODE_DEV)
    picked = table[index].astype(jnp.float32)
    mean_two = (jnp.sum(picked, axis=1) / FAN).astype(jnp.bfloat16)
    target_ids = (jnp.arange(TARGETS, dtype=jnp.int32) // TGT_DEV) * NODE_DEV + jnp.arange(TARGETS, dtype=jnp.int32) % TGT_DEV
    own_rows = hidden_one[target_ids]
    out = jnp.dot(own_rows, self_two, preferred_element_type=jnp.float32) + jnp.dot(mean_two, neigh_two, preferred_element_type=jnp.float32)
    return out.astype(jnp.bfloat16).T
```

```python
import math

import jax
import jax.numpy as jnp
from jax import lax
from jax.sharding import PartitionSpec as P


def left_product(weight, columns):
    return lax.dot_general(
        weight, columns, (((0,), (0,)), ((), ())), preferred_element_type=jnp.float32
    )


def pick_columns(data, index):
    width, extent = data.shape
    count = index.shape[0]
    block = math.gcd(count, 2048)
    blocks = index.reshape(count // block, block)
    places = jnp.arange(extent, dtype=jnp.int32)[:, None]

    def one_block(chosen):
        onehot = (places == chosen[None, :]).astype(data.dtype)
        return jnp.dot(data, onehot, preferred_element_type=jnp.float32).astype(data.dtype)

    picked = lax.map(one_block, blocks)
    return picked.transpose(1, 0, 2).reshape(width, count)


def add_columns(values, index, weight, extent):
    width, count = values.shape
    block = math.gcd(count, 2048)
    nblocks = count // block
    value_blocks = values.reshape(width, nblocks, block).transpose(1, 0, 2)
    index_blocks = index.reshape(nblocks, block)
    weight_blocks = weight.reshape(nblocks, block)
    places = jnp.arange(extent, dtype=jnp.int32)[None, :]

    def step(total, pieces):
        piece, chosen, scale = pieces
        marks = jnp.where(chosen[:, None] == places, scale[:, None], 0.0)
        piece = jnp.concatenate([piece, jnp.ones((1, block), piece.dtype)], axis=0)
        total = total + jnp.dot(
            piece, marks.astype(piece.dtype), preferred_element_type=jnp.float32
        )
        return (total, None)

    start = jnp.zeros((width + 1, extent), jnp.float32)
    total, _ = lax.scan(step, start, (value_blocks, index_blocks, weight_blocks))
    return (total[:width], total[width])


def body(
    features,
    edge_source,
    edge_target,
    edge_count,
    hub_local,
    second_source,
    self_one,
    neigh_one,
    self_two,
    neigh_two,
):
    n_feat = lax.axis_size("feat")
    n_dom = lax.axis_size("dom")
    column_index = lax.axis_index("feat")
    narrow, node_dev = features.shape
    sources = edge_source[0]
    slots = sources.shape[1]
    targets = edge_target[:, 0, :]
    counts = edge_count[:, 0]
    live = (jnp.arange(slots, dtype=jnp.int32)[None, :] < counts[:, None]).astype(jnp.float32)
    chosen = pick_columns(features, sources.reshape(-1)).reshape(narrow, n_dom, slots)
    received = lax.all_to_all(chosen, "dom", split_axis=1, concat_axis=1, tiled=True)
    neighbor_total, degree = add_columns(
        received.reshape(narrow, -1), targets.reshape(-1), live.reshape(-1), node_dev
    )
    mean_one = (neighbor_total / jnp.maximum(degree, 1.0)[None, :]).astype(jnp.bfloat16)
    hidden = self_one.shape[1]
    hcols = hidden // n_feat
    own_all, mean_all = (
        lax.all_gather(features, "feat", axis=0, tiled=True),
        lax.all_gather(mean_one, "feat", axis=0, tiled=True),
    )
    w_own = lax.dynamic_slice_in_dim(self_one, column_index * hcols, hcols, 1)
    w_near = lax.dynamic_slice_in_dim(neigh_one, column_index * hcols, hcols, 1)
    pre_one = left_product(w_own, own_all) + left_product(w_near, mean_all)
    hidden_one = jnp.maximum(pre_one, 0.0).astype(jnp.bfloat16)
    hub_table = lax.all_gather(hidden_one[:, hub_local[0]], "dom", axis=1, tiled=True)
    table = jnp.concatenate([hidden_one, hub_table], axis=1)
    tgt_dev, fanout = second_source.shape
    places = jnp.arange(table.shape[1], dtype=jnp.int32)[:, None]
    tally = jnp.zeros((table.shape[1], tgt_dev), jnp.bfloat16)
    for column in range(fanout):
        tally = tally + (places == second_source[:, column][None, :]).astype(jnp.bfloat16)
    total = jnp.dot(table, tally, preferred_element_type=jnp.float32)
    mean_two = (total / fanout).astype(jnp.bfloat16)
    own_rows = hidden_one[:, :tgt_dev]
    both = lax.all_gather(jnp.stack([own_rows, mean_two]), "feat", axis=1, tiled=True)
    own_wide, mean_wide = both[0], both[1]
    v_own = lax.dynamic_slice_in_dim(self_two, column_index * hcols, hcols, 1)
    v_near = lax.dynamic_slice_in_dim(neigh_two, column_index * hcols, hcols, 1)
    result = left_product(v_own, own_wide) + left_product(v_near, mean_wide)
    return result.astype(jnp.bfloat16)


def solution(mesh):
    return jax.shard_map(
        body,
        mesh=mesh,
        in_specs=(
            P("feat", "dom"),
            P("dom", None, None),
            P(None, "dom", None),
            P(None, "dom"),
            P("dom", None),
            P("dom", None),
            P(),
            P(),
            P(),
            P(),
        ),
        out_specs=P("feat", "dom"),
        check_vma=False,
    )
```

```python
import math

import jax
import jax.numpy as jnp
from jax import lax
from jax.sharding import PartitionSpec as P


def left_product(weight, columns):
    return lax.dot_general(
        weight, columns, (((0,), (0,)), ((), ())), preferred_element_type=jnp.float32
    )


def pick_columns(data, index):
    width, extent = data.shape
    count = index.shape[0]
    block = math.gcd(count, 2048)
    blocks = index.reshape(count // block, block)
    places = jnp.arange(extent, dtype=jnp.int32)[None, :]

    def one_block(chosen):
        onehot = (chosen[:, None] == places).astype(data.dtype)
        return lax.dot_general(
            data, onehot, (((1,), (1,)), ((), ())), preferred_element_type=jnp.float32
        ).astype(data.dtype)

    picked = lax.map(one_block, blocks)
    return picked.transpose(1, 0, 2).reshape(width, count)


def add_columns(values, index, weight, extent):
    width, count = values.shape
    block = math.gcd(count, 2048)
    nblocks = count // block
    value_blocks = values.reshape(width, nblocks, block).transpose(1, 0, 2)
    index_blocks = index.reshape(nblocks, block)
    weight_blocks = weight.reshape(nblocks, block)
    places = jnp.arange(extent, dtype=jnp.int32)[None, :]

    def step(total, pieces):
        piece, chosen, scale = pieces
        marks = jnp.where(chosen[:, None] == places, scale[:, None], 0.0)
        piece = jnp.concatenate([piece, jnp.ones((1, block), piece.dtype)], axis=0)
        total = total + jnp.dot(
            piece, marks.astype(piece.dtype), preferred_element_type=jnp.float32
        )
        return (total, None)

    start = jnp.zeros((width + 1, extent), jnp.float32)
    total, _ = lax.scan(step, start, (value_blocks, index_blocks, weight_blocks))
    return (total[:width], total[width])


def body(
    features,
    edge_source,
    edge_target,
    edge_count,
    hub_local,
    second_source,
    self_one,
    neigh_one,
    self_two,
    neigh_two,
):
    n_feat = lax.axis_size("feat")
    n_dom = lax.axis_size("dom")
    column_index = lax.axis_index("feat")
    narrow, node_dev = features.shape
    sources = edge_source[0]
    slots = sources.shape[1]
    targets = edge_target[:, 0, :]
    counts = edge_count[:, 0]
    live = (jnp.arange(slots, dtype=jnp.int32)[None, :] < counts[:, None]).astype(jnp.float32)
    chosen = pick_columns(features, sources.reshape(-1)).reshape(narrow, n_dom, slots)
    received = lax.all_to_all(chosen, "dom", split_axis=1, concat_axis=1, tiled=True)
    neighbor_total, degree = add_columns(
        received.reshape(narrow, -1), targets.reshape(-1), live.reshape(-1), node_dev
    )
    mean_one = (neighbor_total / jnp.maximum(degree, 1.0)[None, :]).astype(jnp.bfloat16)
    hidden = self_one.shape[1]
    hcols = hidden // n_feat
    own_all, mean_all = (
        lax.all_gather(features, "feat", axis=0, tiled=True),
        lax.all_gather(mean_one, "feat", axis=0, tiled=True),
    )
    w_own = lax.dynamic_slice_in_dim(self_one, column_index * hcols, hcols, 1)
    w_near = lax.dynamic_slice_in_dim(neigh_one, column_index * hcols, hcols, 1)
    pre_one = left_product(w_own, own_all) + left_product(w_near, mean_all)
    hidden_one = jnp.maximum(pre_one, 0.0).astype(jnp.bfloat16)
    hub_table = lax.all_gather(hidden_one[:, hub_local[0]], "dom", axis=1, tiled=True)
    table = jnp.concatenate([hidden_one, hub_table], axis=1)
    tgt_dev, fanout = second_source.shape
    places = jnp.arange(table.shape[1], dtype=jnp.int32)[:, None]
    tally = jnp.zeros((table.shape[1], tgt_dev), jnp.bfloat16)
    for column in range(fanout):
        tally = tally + (places == second_source[:, column][None, :]).astype(jnp.bfloat16)
    total = jnp.dot(table, tally, preferred_element_type=jnp.float32)
    mean_two = (total / fanout).astype(jnp.bfloat16)
    own_rows = hidden_one[:, :tgt_dev]
    both = lax.all_gather(jnp.stack([own_rows, mean_two]), "feat", axis=1, tiled=True)
    own_wide, mean_wide = both[0], both[1]
    v_own = lax.dynamic_slice_in_dim(self_two, column_index * hcols, hcols, 1)
    v_near = lax.dynamic_slice_in_dim(neigh_two, column_index * hcols, hcols, 1)
    result = left_product(v_own, own_wide) + left_product(v_near, mean_wide)
    return result.astype(jnp.bfloat16)


def solution(mesh):
    return jax.shard_map(
        body,
        mesh=mesh,
        in_specs=(
            P("feat", "dom"),
            P("dom", None, None),
            P(None, "dom", None),
            P(None, "dom"),
            P("dom", None),
            P("dom", None),
            P(),
            P(),
            P(),
            P(),
        ),
        out_specs=P("feat", "dom"),
        check_vma=False,
    )
```

```python
import math

import jax
import jax.numpy as jnp
from jax import lax
from jax.sharding import PartitionSpec as P


def left_product(weight, columns):
    return lax.dot_general(
        weight, columns, (((0,), (0,)), ((), ())), preferred_element_type=jnp.float32
    )


def pick_columns(data, index):
    width, extent = data.shape
    count = index.shape[0]
    block = math.gcd(count, 2048)
    blocks = index.reshape(count // block, block)
    places = jnp.arange(extent, dtype=jnp.int32)[:, None]

    def one_block(chosen):
        onehot = (places == chosen[None, :]).astype(data.dtype)
        return jnp.dot(data, onehot, preferred_element_type=jnp.float32).astype(data.dtype)

    picked = lax.map(one_block, blocks)
    return picked.transpose(1, 0, 2).reshape(width, count)


def add_columns(values, index, weight, extent):
    width, count = values.shape
    block = math.gcd(count, 2048)
    nblocks = count // block
    value_blocks = values.reshape(width, nblocks, block).transpose(1, 0, 2)
    index_blocks = index.reshape(nblocks, block)
    weight_blocks = weight.reshape(nblocks, block)
    places = jnp.arange(extent, dtype=jnp.int32)[None, :]

    def step(total, pieces):
        piece, chosen, scale = pieces
        marks = jnp.where(chosen[:, None] == places, scale[:, None], 0.0)
        piece = jnp.concatenate([piece, jnp.ones((1, block), piece.dtype)], axis=0)
        total = total + jnp.dot(
            piece, marks.astype(piece.dtype), preferred_element_type=jnp.float32
        )
        return (total, None)

    start = jnp.zeros((width + 1, extent), jnp.float32)
    total, _ = lax.scan(step, start, (value_blocks, index_blocks, weight_blocks))
    return (total[:width], total[width])


def body(
    features,
    edge_source,
    edge_target,
    edge_count,
    hub_local,
    second_source,
    self_one,
    neigh_one,
    self_two,
    neigh_two,
):
    n_feat = lax.axis_size("feat")
    n_dom = lax.axis_size("dom")
    column_index = lax.axis_index("feat")
    narrow, node_dev = features.shape
    sources = edge_source[0]
    slots = sources.shape[1]
    targets = edge_target[:, 0, :]
    counts = edge_count[:, 0]
    live = (jnp.arange(slots, dtype=jnp.int32)[None, :] < counts[:, None]).astype(jnp.float32)
    chosen = pick_columns(features, sources.reshape(-1)).reshape(narrow, n_dom, slots)
    received = lax.all_to_all(chosen, "dom", split_axis=1, concat_axis=1, tiled=True)
    neighbor_total, degree = add_columns(
        received.reshape(narrow, -1), targets.reshape(-1), live.reshape(-1), node_dev
    )
    mean_one = (neighbor_total / jnp.maximum(degree, 1.0)[None, :]).astype(jnp.bfloat16)
    hidden = self_one.shape[1]
    hcols = hidden // n_feat
    own_all, mean_all = (
        lax.all_gather(features, "feat", axis=0, tiled=True),
        lax.all_gather(mean_one, "feat", axis=0, tiled=True),
    )
    w_own = lax.dynamic_slice_in_dim(self_one, column_index * hcols, hcols, 1)
    w_near = lax.dynamic_slice_in_dim(neigh_one, column_index * hcols, hcols, 1)
    pre_one = left_product(w_own, own_all) + left_product(w_near, mean_all)
    hidden_one = jnp.maximum(pre_one, 0.0).astype(jnp.bfloat16)
    hub_rows = hidden_one[:, hub_local[0]]
    hub_count = hub_rows.shape[1]
    spread = jnp.broadcast_to(hub_rows[None], (n_dom,) + hub_rows.shape)
    landed = lax.all_to_all(spread, "dom", split_axis=0, concat_axis=0, tiled=True)
    hub_table = landed.transpose(1, 0, 2).reshape(hidden_one.shape[0], n_dom * hub_count)
    tgt_dev, fanout = second_source.shape
    near_places = jnp.arange(node_dev, dtype=jnp.int32)[:, None]
    hub_places = node_dev + jnp.arange(n_dom * hub_count, dtype=jnp.int32)[:, None]
    near_tally = jnp.zeros((node_dev, tgt_dev), jnp.bfloat16)
    hub_tally = jnp.zeros((n_dom * hub_count, tgt_dev), jnp.bfloat16)
    for column in range(fanout):
        picked = second_source[:, column][None, :]
        near_tally = near_tally + (near_places == picked).astype(jnp.bfloat16)
        hub_tally = hub_tally + (hub_places == picked).astype(jnp.bfloat16)
    total = jnp.dot(hidden_one, near_tally, preferred_element_type=jnp.float32)
    total = total + jnp.dot(hub_table, hub_tally, preferred_element_type=jnp.float32)
    mean_two = (total / fanout).astype(jnp.bfloat16)
    own_rows = hidden_one[:, :tgt_dev]
    both = lax.all_gather(jnp.stack([own_rows, mean_two]), "feat", axis=1, tiled=True)
    own_wide, mean_wide = both[0], both[1]
    v_own = lax.dynamic_slice_in_dim(self_two, column_index * hcols, hcols, 1)
    v_near = lax.dynamic_slice_in_dim(neigh_two, column_index * hcols, hcols, 1)
    result = left_product(v_own, own_wide) + left_product(v_near, mean_wide)
    return result.astype(jnp.bfloat16)


def solution(mesh):
    return jax.shard_map(
        body,
        mesh=mesh,
        in_specs=(
            P("feat", "dom"),
            P("dom", None, None),
            P(None, "dom", None),
            P(None, "dom"),
            P("dom", None),
            P("dom", None),
            P(),
            P(),
            P(),
            P(),
        ),
        out_specs=P("feat", "dom"),
        check_vma=False,
    )
```

```python
import math

import jax
import jax.numpy as jnp
from jax import lax
from jax.sharding import PartitionSpec as P


def left_product(weight, columns):
    return lax.dot_general(
        weight, columns, (((0,), (0,)), ((), ())), preferred_element_type=jnp.float32
    )


def pick_columns(data, index):
    width, extent = data.shape
    count = index.shape[0]
    block = math.gcd(count, 2048)
    blocks = index.reshape(count // block, block)
    places = jnp.arange(extent, dtype=jnp.int32)[:, None]

    def one_block(chosen):
        onehot = (places == chosen[None, :]).astype(data.dtype)
        return jnp.dot(data, onehot, preferred_element_type=jnp.float32).astype(data.dtype)

    picked = lax.map(one_block, blocks)
    return picked.transpose(1, 0, 2).reshape(width, count)


def add_columns(values, index, weight, extent):
    width, count = values.shape
    block = math.gcd(count, 2048)
    nblocks = count // block
    value_blocks = values.reshape(width, nblocks, block).transpose(1, 0, 2)
    index_blocks = index.reshape(nblocks, block)
    weight_blocks = weight.reshape(nblocks, block)
    places = jnp.arange(extent, dtype=jnp.int32)[None, :]

    def step(total, pieces):
        piece, chosen, scale = pieces
        marks = jnp.where(chosen[:, None] == places, scale[:, None], 0.0)
        piece = jnp.concatenate([piece, jnp.ones((1, block), piece.dtype)], axis=0)
        total = total + jnp.dot(
            piece, marks.astype(piece.dtype), preferred_element_type=jnp.float32
        )
        return (total, None)

    start = jnp.zeros((width + 1, extent), jnp.float32)
    total, _ = lax.scan(step, start, (value_blocks, index_blocks, weight_blocks))
    return (total[:width], total[width])


def body(
    features,
    edge_source,
    edge_target,
    edge_count,
    hub_local,
    second_source,
    self_one,
    neigh_one,
    self_two,
    neigh_two,
):
    n_feat = lax.axis_size("feat")
    n_dom = lax.axis_size("dom")
    column_index = lax.axis_index("feat")
    narrow, node_dev = features.shape
    sources = edge_source[0]
    slots = sources.shape[1]
    targets = edge_target[:, 0, :]
    counts = edge_count[:, 0]
    live = (jnp.arange(slots, dtype=jnp.int32)[None, :] < counts[:, None]).astype(jnp.float32)
    chunks = 2
    piece = slots // chunks
    neighbor_total, degree = 0.0, 0.0
    for part in range(chunks):
        cut = slice(part * piece, (part + 1) * piece)
        chosen = pick_columns(features, sources[:, cut].reshape(-1)).reshape(narrow, n_dom, piece)
        received = lax.all_to_all(chosen, "dom", split_axis=1, concat_axis=1, tiled=True)
        part_total, part_degree = add_columns(
            received.reshape(narrow, -1), targets[:, cut].reshape(-1), live[:, cut].reshape(-1), node_dev
        )
        neighbor_total = neighbor_total + part_total
        degree = degree + part_degree
    mean_one = (neighbor_total / jnp.maximum(degree, 1.0)[None, :]).astype(jnp.bfloat16)
    hidden = self_one.shape[1]
    hcols = hidden // n_feat
    own_all, mean_all = (
        lax.all_gather(features, "feat", axis=0, tiled=True),
        lax.all_gather(mean_one, "feat", axis=0, tiled=True),
    )
    w_own = lax.dynamic_slice_in_dim(self_one, column_index * hcols, hcols, 1)
    w_near = lax.dynamic_slice_in_dim(neigh_one, column_index * hcols, hcols, 1)
    pre_one = left_product(w_own, own_all) + left_product(w_near, mean_all)
    hidden_one = jnp.maximum(pre_one, 0.0).astype(jnp.bfloat16)
    hub_rows = hidden_one[:, hub_local[0]]
    hub_count = hub_rows.shape[1]
    spread = jnp.broadcast_to(hub_rows[None], (n_dom,) + hub_rows.shape)
    landed = lax.all_to_all(spread, "dom", split_axis=0, concat_axis=0, tiled=True)
    hub_table = landed.transpose(1, 0, 2).reshape(hidden_one.shape[0], n_dom * hub_count)
    tgt_dev, fanout = second_source.shape
    near_places = jnp.arange(node_dev, dtype=jnp.int32)[:, None]
    hub_places = node_dev + jnp.arange(n_dom * hub_count, dtype=jnp.int32)[:, None]
    near_tally = jnp.zeros((node_dev, tgt_dev), jnp.bfloat16)
    hub_tally = jnp.zeros((n_dom * hub_count, tgt_dev), jnp.bfloat16)
    for column in range(fanout):
        picked = second_source[:, column][None, :]
        near_tally = near_tally + (near_places == picked).astype(jnp.bfloat16)
        hub_tally = hub_tally + (hub_places == picked).astype(jnp.bfloat16)
    total = jnp.dot(hidden_one, near_tally, preferred_element_type=jnp.float32)
    total = total + jnp.dot(hub_table, hub_tally, preferred_element_type=jnp.float32)
    mean_two = (total / fanout).astype(jnp.bfloat16)
    own_cols = lax.dynamic_slice_in_dim(own_all, 0, tgt_dev, 1)
    near_cols = lax.dynamic_slice_in_dim(mean_all, 0, tgt_dev, 1)
    own_wide = jnp.maximum(
        left_product(self_one, own_cols) + left_product(neigh_one, near_cols), 0.0
    ).astype(jnp.bfloat16)
    mean_wide = lax.all_gather(mean_two, "feat", axis=0, tiled=True)
    v_own = lax.dynamic_slice_in_dim(self_two, column_index * hcols, hcols, 1)
    v_near = lax.dynamic_slice_in_dim(neigh_two, column_index * hcols, hcols, 1)
    result = left_product(v_own, own_wide) + left_product(v_near, mean_wide)
    return result.astype(jnp.bfloat16)


def solution(mesh):
    return jax.shard_map(
        body,
        mesh=mesh,
        in_specs=(
            P("feat", "dom"),
            P("dom", None, None),
            P(None, "dom", None),
            P(None, "dom"),
            P("dom", None),
            P("dom", None),
            P(),
            P(),
            P(),
            P(),
        ),
        out_specs=P("feat", "dom"),
        check_vma=False,
    )
```

```python
import math

import jax
import jax.numpy as jnp
from jax import lax
from jax.sharding import PartitionSpec as P


def left_product(weight, columns):
    return lax.dot_general(
        weight, columns, (((0,), (0,)), ((), ())), preferred_element_type=jnp.float32
    )


def pick_columns(data, index):
    width, extent = data.shape
    count = index.shape[0]
    block = math.gcd(count, 2048)
    blocks = index.reshape(count // block, block)
    places = jnp.arange(extent, dtype=jnp.int32)[:, None]

    def one_block(chosen):
        onehot = (places == chosen[None, :]).astype(data.dtype)
        return jnp.dot(data, onehot, preferred_element_type=jnp.float32).astype(data.dtype)

    picked = lax.map(one_block, blocks)
    return picked.transpose(1, 0, 2).reshape(width, count)


def add_columns(values, index, weight, extent):
    width, count = values.shape
    block = math.gcd(count, 2048)
    nblocks = count // block
    value_blocks = values.reshape(width, nblocks, block).transpose(1, 0, 2)
    index_blocks = index.reshape(nblocks, block)
    weight_blocks = weight.reshape(nblocks, block)
    places = jnp.arange(extent, dtype=jnp.int32)[None, :]

    def step(total, pieces):
        piece, chosen, scale = pieces
        marks = jnp.where(chosen[:, None] == places, scale[:, None], 0.0)
        piece = jnp.concatenate([piece, jnp.ones((1, block), piece.dtype)], axis=0)
        total = total + jnp.dot(
            piece, marks.astype(piece.dtype), preferred_element_type=jnp.float32
        )
        return (total, None)

    start = jnp.zeros((width + 1, extent), jnp.float32)
    total, _ = lax.scan(step, start, (value_blocks, index_blocks, weight_blocks))
    return (total[:width], total[width])


def body(
    features,
    edge_source,
    edge_target,
    edge_count,
    hub_local,
    second_source,
    self_one,
    neigh_one,
    self_two,
    neigh_two,
):
    n_feat = lax.axis_size("feat")
    n_dom = lax.axis_size("dom")
    column_index = lax.axis_index("feat")
    narrow, node_dev = features.shape
    sources = edge_source[0]
    slots = sources.shape[1]
    targets = edge_target[:, 0, :]
    counts = edge_count[:, 0]
    live = (jnp.arange(slots, dtype=jnp.int32)[None, :] < counts[:, None]).astype(jnp.float32)
    chosen = pick_columns(features, sources.reshape(-1)).reshape(narrow, n_dom, slots)
    received = lax.all_to_all(chosen, "dom", split_axis=1, concat_axis=1, tiled=True)
    neighbor_total, degree = add_columns(
        received.reshape(narrow, -1), targets.reshape(-1), live.reshape(-1), node_dev
    )
    mean_one = (neighbor_total / jnp.maximum(degree, 1.0)[None, :]).astype(jnp.bfloat16)
    hidden = self_one.shape[1]
    hcols = hidden // n_feat
    own_all, mean_all = (
        lax.all_gather(features, "feat", axis=0, tiled=True),
        lax.all_gather(mean_one, "feat", axis=0, tiled=True),
    )
    w_own = lax.dynamic_slice_in_dim(self_one, column_index * hcols, hcols, 1)
    w_near = lax.dynamic_slice_in_dim(neigh_one, column_index * hcols, hcols, 1)
    pre_one = left_product(w_own, own_all) + left_product(w_near, mean_all)
    hidden_one = jnp.maximum(pre_one, 0.0).astype(jnp.bfloat16)
    hub_rows = hidden_one[:, hub_local[0]]
    hub_count = hub_rows.shape[1]
    spread = jnp.broadcast_to(hub_rows[None], (n_dom,) + hub_rows.shape)
    landed = lax.all_to_all(spread, "dom", split_axis=0, concat_axis=0, tiled=True)
    hub_table = landed.transpose(1, 0, 2).reshape(hidden_one.shape[0], n_dom * hub_count)
    tgt_dev, fanout = second_source.shape
    near_places = jnp.arange(node_dev, dtype=jnp.int32)[:, None]
    hub_places = node_dev + jnp.arange(n_dom * hub_count, dtype=jnp.int32)[:, None]
    near_tally = jnp.zeros((node_dev, tgt_dev), jnp.bfloat16)
    hub_tally = jnp.zeros((n_dom * hub_count, tgt_dev), jnp.bfloat16)
    for column in range(fanout):
        picked = second_source[:, column][None, :]
        near_tally = near_tally + (near_places == picked).astype(jnp.bfloat16)
        hub_tally = hub_tally + (hub_places == picked).astype(jnp.bfloat16)
    near_tally, hub_tally = lax.optimization_barrier((near_tally, hub_tally))
    total = jnp.dot(hidden_one, near_tally, preferred_element_type=jnp.float32)
    total = total + jnp.dot(hub_table, hub_tally, preferred_element_type=jnp.float32)
    mean_two = (total / fanout).astype(jnp.bfloat16)
    own_cols = lax.dynamic_slice_in_dim(own_all, 0, tgt_dev, 1)
    near_cols = lax.dynamic_slice_in_dim(mean_all, 0, tgt_dev, 1)
    own_wide = jnp.maximum(
        left_product(self_one, own_cols) + left_product(neigh_one, near_cols), 0.0
    ).astype(jnp.bfloat16)
    mean_wide = lax.all_gather(mean_two, "feat", axis=0, tiled=True)
    v_own = lax.dynamic_slice_in_dim(self_two, column_index * hcols, hcols, 1)
    v_near = lax.dynamic_slice_in_dim(neigh_two, column_index * hcols, hcols, 1)
    result = left_product(v_own, own_wide) + left_product(v_near, mean_wide)
    return result.astype(jnp.bfloat16)


def solution(mesh):
    return jax.shard_map(
        body,
        mesh=mesh,
        in_specs=(
            P("feat", "dom"),
            P("dom", None, None),
            P(None, "dom", None),
            P(None, "dom"),
            P("dom", None),
            P("dom", None),
            P(),
            P(),
            P(),
            P(),
        ),
        out_specs=P("feat", "dom"),
        check_vma=False,
    )
```

```python
import math

import jax
import jax.numpy as jnp
from jax import lax
from jax.sharding import PartitionSpec as P


def left_product(weight, columns):
    return lax.dot_general(
        weight, columns, (((0,), (0,)), ((), ())), preferred_element_type=jnp.float32
    )


def pick_columns(data, index):
    extent = data.shape[1]
    places = jnp.arange(extent, dtype=jnp.int32)[:, None]
    onehot = (places == index[None, :]).astype(data.dtype)
    return jnp.dot(data, onehot, preferred_element_type=jnp.float32).astype(data.dtype)


def add_columns(values, index, weight, extent):
    width, count = values.shape
    places = jnp.arange(extent, dtype=jnp.int32)[None, :]
    marks = jnp.where(index[:, None] == places, weight[:, None], 0.0).astype(values.dtype)
    values = jnp.concatenate([values, jnp.ones((1, count), values.dtype)], axis=0)
    total = jnp.dot(values, marks, preferred_element_type=jnp.float32)
    return (total[:width], total[width])


def body(
    features,
    edge_source,
    edge_target,
    edge_count,
    hub_local,
    second_source,
    self_one,
    neigh_one,
    self_two,
    neigh_two,
):
    n_feat = lax.axis_size("feat")
    n_dom = lax.axis_size("dom")
    column_index = lax.axis_index("feat")
    narrow, node_dev = features.shape
    sources = edge_source[0]
    slots = sources.shape[1]
    targets = edge_target[:, 0, :]
    counts = edge_count[:, 0]
    live = (jnp.arange(slots, dtype=jnp.int32)[None, :] < counts[:, None]).astype(jnp.float32)
    chosen = pick_columns(features, sources.reshape(-1)).reshape(narrow, n_dom, slots)
    received = lax.all_to_all(chosen, "dom", split_axis=1, concat_axis=1, tiled=True)
    neighbor_total, degree = add_columns(
        received.reshape(narrow, -1), targets.reshape(-1), live.reshape(-1), node_dev
    )
    mean_one = (neighbor_total / jnp.maximum(degree, 1.0)[None, :]).astype(jnp.bfloat16)
    hidden = self_one.shape[1]
    hcols = hidden // n_feat
    own_all, mean_all = (
        lax.all_gather(features, "feat", axis=0, tiled=True),
        lax.all_gather(mean_one, "feat", axis=0, tiled=True),
    )
    w_own = lax.dynamic_slice_in_dim(self_one, column_index * hcols, hcols, 1)
    w_near = lax.dynamic_slice_in_dim(neigh_one, column_index * hcols, hcols, 1)
    pre_one = left_product(w_own, own_all) + left_product(w_near, mean_all)
    hidden_one = jnp.maximum(pre_one, 0.0).astype(jnp.bfloat16)
    hub_rows = hidden_one[:, hub_local[0]]
    hub_count = hub_rows.shape[1]
    spread = jnp.broadcast_to(hub_rows[None], (n_dom,) + hub_rows.shape)
    landed = lax.all_to_all(spread, "dom", split_axis=0, concat_axis=0, tiled=True)
    hub_table = landed.transpose(1, 0, 2).reshape(hidden_one.shape[0], n_dom * hub_count)
    tgt_dev, fanout = second_source.shape
    near_places = jnp.arange(node_dev, dtype=jnp.int32)[:, None]
    hub_places = node_dev + jnp.arange(n_dom * hub_count, dtype=jnp.int32)[:, None]
    near_tally = jnp.zeros((node_dev, tgt_dev), jnp.bfloat16)
    hub_tally = jnp.zeros((n_dom * hub_count, tgt_dev), jnp.bfloat16)
    for column in range(fanout):
        picked = second_source[:, column][None, :]
        near_tally = near_tally + (near_places == picked).astype(jnp.bfloat16)
        hub_tally = hub_tally + (hub_places == picked).astype(jnp.bfloat16)
    near_tally, hub_tally = lax.optimization_barrier((near_tally, hub_tally))
    total = jnp.dot(hidden_one, near_tally, preferred_element_type=jnp.float32)
    total = total + jnp.dot(hub_table, hub_tally, preferred_element_type=jnp.float32)
    mean_two = (total / fanout).astype(jnp.bfloat16)
    own_cols = lax.dynamic_slice_in_dim(own_all, 0, tgt_dev, 1)
    near_cols = lax.dynamic_slice_in_dim(mean_all, 0, tgt_dev, 1)
    own_wide = jnp.maximum(
        left_product(self_one, own_cols) + left_product(neigh_one, near_cols), 0.0
    ).astype(jnp.bfloat16)
    mean_wide = lax.all_gather(mean_two, "feat", axis=0, tiled=True)
    v_own = lax.dynamic_slice_in_dim(self_two, column_index * hcols, hcols, 1)
    v_near = lax.dynamic_slice_in_dim(neigh_two, column_index * hcols, hcols, 1)
    result = left_product(v_own, own_wide) + left_product(v_near, mean_wide)
    return result.astype(jnp.bfloat16)


def solution(mesh):
    return jax.shard_map(
        body,
        mesh=mesh,
        in_specs=(
            P("feat", "dom"),
            P("dom", None, None),
            P(None, "dom", None),
            P(None, "dom"),
            P("dom", None),
            P("dom", None),
            P(),
            P(),
            P(),
            P(),
        ),
        out_specs=P("feat", "dom"),
        check_vma=False,
    )
```

```python
import math

import jax
import jax.numpy as jnp
from jax import lax
from jax.sharding import PartitionSpec as P


def left_product(weight, columns):
    return lax.dot_general(
        weight, columns, (((0,), (0,)), ((), ())), preferred_element_type=jnp.float32
    )


def pick_columns(data, index):
    return jnp.take(data.T, index, axis=0, mode="clip").T


def add_columns(values, index, weight, extent):
    width, count = values.shape
    places = jnp.arange(extent, dtype=jnp.int32)[None, :]
    marks = jnp.where(index[:, None] == places, weight[:, None], 0.0).astype(values.dtype)
    values = jnp.concatenate([values, jnp.ones((1, count), values.dtype)], axis=0)
    total = jnp.dot(values, marks, preferred_element_type=jnp.float32)
    return (total[:width], total[width])


def body(
    features,
    edge_source,
    edge_target,
    edge_count,
    hub_local,
    second_source,
    self_one,
    neigh_one,
    self_two,
    neigh_two,
):
    n_feat = lax.axis_size("feat")
    n_dom = lax.axis_size("dom")
    column_index = lax.axis_index("feat")
    narrow, node_dev = features.shape
    sources = edge_source[0]
    slots = sources.shape[1]
    targets = edge_target[:, 0, :]
    counts = edge_count[:, 0]
    live = (jnp.arange(slots, dtype=jnp.int32)[None, :] < counts[:, None]).astype(jnp.float32)
    chosen = pick_columns(features, sources.reshape(-1)).reshape(narrow, n_dom, slots)
    received = lax.all_to_all(chosen, "dom", split_axis=1, concat_axis=1, tiled=True)
    neighbor_total, degree = add_columns(
        received.reshape(narrow, -1), targets.reshape(-1), live.reshape(-1), node_dev
    )
    mean_one = (neighbor_total / jnp.maximum(degree, 1.0)[None, :]).astype(jnp.bfloat16)
    hidden = self_one.shape[1]
    hcols = hidden // n_feat
    own_all, mean_all = (
        lax.all_gather(features, "feat", axis=0, tiled=True),
        lax.all_gather(mean_one, "feat", axis=0, tiled=True),
    )
    w_own = lax.dynamic_slice_in_dim(self_one, column_index * hcols, hcols, 1)
    w_near = lax.dynamic_slice_in_dim(neigh_one, column_index * hcols, hcols, 1)
    pre_one = left_product(w_own, own_all) + left_product(w_near, mean_all)
    hidden_one = jnp.maximum(pre_one, 0.0).astype(jnp.bfloat16)
    hub_rows = hidden_one[:, hub_local[0]]
    hub_count = hub_rows.shape[1]
    spread = jnp.broadcast_to(hub_rows[None], (n_dom,) + hub_rows.shape)
    landed = lax.all_to_all(spread, "dom", split_axis=0, concat_axis=0, tiled=True)
    hub_table = landed.transpose(1, 0, 2).reshape(hidden_one.shape[0], n_dom * hub_count)
    tgt_dev, fanout = second_source.shape
    near_places = jnp.arange(node_dev, dtype=jnp.int32)[:, None]
    hub_places = node_dev + jnp.arange(n_dom * hub_count, dtype=jnp.int32)[:, None]
    near_tally = jnp.zeros((node_dev, tgt_dev), jnp.bfloat16)
    hub_tally = jnp.zeros((n_dom * hub_count, tgt_dev), jnp.bfloat16)
    for column in range(fanout):
        picked = second_source[:, column][None, :]
        near_tally = near_tally + (near_places == picked).astype(jnp.bfloat16)
        hub_tally = hub_tally + (hub_places == picked).astype(jnp.bfloat16)
    near_tally, hub_tally = lax.optimization_barrier((near_tally, hub_tally))
    total = jnp.dot(hidden_one, near_tally, preferred_element_type=jnp.float32)
    total = total + jnp.dot(hub_table, hub_tally, preferred_element_type=jnp.float32)
    mean_two = (total / fanout).astype(jnp.bfloat16)
    own_cols = lax.dynamic_slice_in_dim(own_all, 0, tgt_dev, 1)
    near_cols = lax.dynamic_slice_in_dim(mean_all, 0, tgt_dev, 1)
    own_wide = jnp.maximum(
        left_product(self_one, own_cols) + left_product(neigh_one, near_cols), 0.0
    ).astype(jnp.bfloat16)
    mean_wide = lax.all_gather(mean_two, "feat", axis=0, tiled=True)
    v_own = lax.dynamic_slice_in_dim(self_two, column_index * hcols, hcols, 1)
    v_near = lax.dynamic_slice_in_dim(neigh_two, column_index * hcols, hcols, 1)
    result = left_product(v_own, own_wide) + left_product(v_near, mean_wide)
    return result.astype(jnp.bfloat16)


def solution(mesh):
    return jax.shard_map(
        body,
        mesh=mesh,
        in_specs=(
            P("feat", "dom"),
            P("dom", None, None),
            P(None, "dom", None),
            P(None, "dom"),
            P("dom", None),
            P("dom", None),
            P(),
            P(),
            P(),
            P(),
        ),
        out_specs=P("feat", "dom"),
        check_vma=False,
    )
```

```python
import math

import jax
import jax.numpy as jnp
from jax import lax
from jax.sharding import PartitionSpec as P


def left_product(weight, columns):
    return lax.dot_general(
        weight, columns, (((0,), (0,)), ((), ())), preferred_element_type=jnp.float32
    )


def pick_columns(data, index):
    extent = data.shape[1]
    places = jnp.arange(extent, dtype=jnp.int16)[:, None]
    onehot = (places == index.astype(jnp.int16)[None, :]).astype(data.dtype)
    return jnp.dot(data, onehot, preferred_element_type=jnp.float32).astype(data.dtype)


def add_columns(values, index, weight, extent):
    width, count = values.shape
    places = jnp.arange(extent, dtype=jnp.int16)[None, :]
    marks = jnp.where(
        index.astype(jnp.int16)[:, None] == places, weight.astype(values.dtype)[:, None], 0.0
    ).astype(values.dtype)
    values = jnp.concatenate([values, jnp.ones((1, count), values.dtype)], axis=0)
    total = jnp.dot(values, marks, preferred_element_type=jnp.float32)
    return (total[:width], total[width])


def body(
    features,
    edge_source,
    edge_target,
    edge_count,
    hub_local,
    second_source,
    self_one,
    neigh_one,
    self_two,
    neigh_two,
):
    n_feat = lax.axis_size("feat")
    n_dom = lax.axis_size("dom")
    column_index = lax.axis_index("feat")
    narrow, node_dev = features.shape
    sources = edge_source[0]
    slots = sources.shape[1]
    targets = edge_target[:, 0, :]
    counts = edge_count[:, 0]
    live = (jnp.arange(slots, dtype=jnp.int32)[None, :] < counts[:, None]).astype(jnp.float32)
    chosen = pick_columns(features, sources.reshape(-1)).reshape(narrow, n_dom, slots)
    received = lax.all_to_all(chosen, "dom", split_axis=1, concat_axis=1, tiled=True)
    neighbor_total, degree = add_columns(
        received.reshape(narrow, -1), targets.reshape(-1), live.reshape(-1), node_dev
    )
    mean_one = (neighbor_total / jnp.maximum(degree, 1.0)[None, :]).astype(jnp.bfloat16)
    hidden = self_one.shape[1]
    hcols = hidden // n_feat
    own_all, mean_all = (
        lax.all_gather(features, "feat", axis=0, tiled=True),
        lax.all_gather(mean_one, "feat", axis=0, tiled=True),
    )
    w_own = lax.dynamic_slice_in_dim(self_one, column_index * hcols, hcols, 1)
    w_near = lax.dynamic_slice_in_dim(neigh_one, column_index * hcols, hcols, 1)
    pre_one = left_product(w_own, own_all) + left_product(w_near, mean_all)
    hidden_one = jnp.maximum(pre_one, 0.0).astype(jnp.bfloat16)
    hub_rows = hidden_one[:, hub_local[0]]
    hub_count = hub_rows.shape[1]
    spread = jnp.broadcast_to(hub_rows[None], (n_dom,) + hub_rows.shape)
    landed = lax.all_to_all(spread, "dom", split_axis=0, concat_axis=0, tiled=True)
    hub_table = landed.transpose(1, 0, 2).reshape(hidden_one.shape[0], n_dom * hub_count)
    tgt_dev, fanout = second_source.shape
    near_places = jnp.arange(node_dev, dtype=jnp.int16)[:, None]
    hub_places = (node_dev + jnp.arange(n_dom * hub_count, dtype=jnp.int32)).astype(jnp.int16)[:, None]
    near_tally = jnp.zeros((node_dev, tgt_dev), jnp.bfloat16)
    hub_tally = jnp.zeros((n_dom * hub_count, tgt_dev), jnp.bfloat16)
    for column in range(fanout):
        picked = second_source[:, column].astype(jnp.int16)[None, :]
        near_tally = near_tally + (near_places == picked).astype(jnp.bfloat16)
        hub_tally = hub_tally + (hub_places == picked).astype(jnp.bfloat16)
    near_tally, hub_tally = lax.optimization_barrier((near_tally, hub_tally))
    total = jnp.dot(hidden_one, near_tally, preferred_element_type=jnp.float32)
    total = total + jnp.dot(hub_table, hub_tally, preferred_element_type=jnp.float32)
    mean_two = (total / fanout).astype(jnp.bfloat16)
    own_cols = lax.dynamic_slice_in_dim(own_all, 0, tgt_dev, 1)
    near_cols = lax.dynamic_slice_in_dim(mean_all, 0, tgt_dev, 1)
    own_wide = jnp.maximum(
        left_product(self_one, own_cols) + left_product(neigh_one, near_cols), 0.0
    ).astype(jnp.bfloat16)
    mean_wide = lax.all_gather(mean_two, "feat", axis=0, tiled=True)
    v_own = lax.dynamic_slice_in_dim(self_two, column_index * hcols, hcols, 1)
    v_near = lax.dynamic_slice_in_dim(neigh_two, column_index * hcols, hcols, 1)
    result = left_product(v_own, own_wide) + left_product(v_near, mean_wide)
    return result.astype(jnp.bfloat16)


def solution(mesh):
    return jax.shard_map(
        body,
        mesh=mesh,
        in_specs=(
            P("feat", "dom"),
            P("dom", None, None),
            P(None, "dom", None),
            P(None, "dom"),
            P("dom", None),
            P("dom", None),
            P(),
            P(),
            P(),
            P(),
        ),
        out_specs=P("feat", "dom"),
        check_vma=False,
    )
```

```python
import math

import jax
import jax.numpy as jnp
from jax import lax
from jax.sharding import PartitionSpec as P


def left_product(weight, columns):
    return lax.dot_general(
        weight, columns, (((0,), (0,)), ((), ())), preferred_element_type=jnp.float32
    )


def pick_columns(data, index, groups=8):
    width, extent = data.shape
    span = extent // groups
    stacked = data.reshape(width, groups, span).transpose(1, 0, 2).reshape(groups * width, span)
    low = (index % span).astype(jnp.int16)
    high = index // span
    places = jnp.arange(span, dtype=jnp.int16)[:, None]
    onehot = (places == low[None, :]).astype(data.dtype)
    rows = jnp.dot(stacked, onehot, preferred_element_type=jnp.float32).astype(data.dtype)
    rows = rows.reshape(groups, width, index.shape[0])
    keep = high[None, None, :] == jnp.arange(groups, dtype=jnp.int32)[:, None, None]
    return jnp.sum(jnp.where(keep, rows, 0), axis=0, dtype=jnp.float32).astype(data.dtype)


def add_columns(values, index, weight, extent, groups=8):
    width, count = values.shape
    span = extent // groups
    values = jnp.concatenate([values, jnp.ones((1, count), values.dtype)], axis=0)
    values = values * weight.astype(values.dtype)[None, :]
    low = (index % span).astype(jnp.int16)
    high = index // span
    keep = high[None, None, :] == jnp.arange(groups, dtype=jnp.int32)[:, None, None]
    spread = jnp.where(keep, values[None], 0).astype(values.dtype).reshape(groups * (width + 1), count)
    places = jnp.arange(span, dtype=jnp.int16)[None, :]
    marks = (low[:, None] == places).astype(values.dtype)
    total = jnp.dot(spread, marks, preferred_element_type=jnp.float32)
    total = total.reshape(groups, width + 1, span).transpose(1, 0, 2).reshape(width + 1, extent)
    return (total[:width], total[width])


def body(
    features,
    edge_source,
    edge_target,
    edge_count,
    hub_local,
    second_source,
    self_one,
    neigh_one,
    self_two,
    neigh_two,
):
    n_feat = lax.axis_size("feat")
    n_dom = lax.axis_size("dom")
    column_index = lax.axis_index("feat")
    narrow, node_dev = features.shape
    sources = edge_source[0]
    slots = sources.shape[1]
    targets = edge_target[:, 0, :]
    counts = edge_count[:, 0]
    live = (jnp.arange(slots, dtype=jnp.int32)[None, :] < counts[:, None]).astype(jnp.float32)
    chosen = pick_columns(features, sources.reshape(-1)).reshape(narrow, n_dom, slots)
    received = lax.all_to_all(chosen, "dom", split_axis=1, concat_axis=1, tiled=True)
    neighbor_total, degree = add_columns(
        received.reshape(narrow, -1), targets.reshape(-1), live.reshape(-1), node_dev
    )
    mean_one = (neighbor_total / jnp.maximum(degree, 1.0)[None, :]).astype(jnp.bfloat16)
    hidden = self_one.shape[1]
    hcols = hidden // n_feat
    own_all, mean_all = (
        lax.all_gather(features, "feat", axis=0, tiled=True),
        lax.all_gather(mean_one, "feat", axis=0, tiled=True),
    )
    w_own = lax.dynamic_slice_in_dim(self_one, column_index * hcols, hcols, 1)
    w_near = lax.dynamic_slice_in_dim(neigh_one, column_index * hcols, hcols, 1)
    pre_one = left_product(w_own, own_all) + left_product(w_near, mean_all)
    hidden_one = jnp.maximum(pre_one, 0.0).astype(jnp.bfloat16)
    hub_rows = hidden_one[:, hub_local[0]]
    hub_count = hub_rows.shape[1]
    spread = jnp.broadcast_to(hub_rows[None], (n_dom,) + hub_rows.shape)
    landed = lax.all_to_all(spread, "dom", split_axis=0, concat_axis=0, tiled=True)
    hub_table = landed.transpose(1, 0, 2).reshape(hidden_one.shape[0], n_dom * hub_count)
    tgt_dev, fanout = second_source.shape
    near_places = jnp.arange(node_dev, dtype=jnp.int16)[:, None]
    hub_places = (node_dev + jnp.arange(n_dom * hub_count, dtype=jnp.int32)).astype(jnp.int16)[:, None]
    near_tally = jnp.zeros((node_dev, tgt_dev), jnp.bfloat16)
    hub_tally = jnp.zeros((n_dom * hub_count, tgt_dev), jnp.bfloat16)
    for column in range(fanout):
        picked = second_source[:, column].astype(jnp.int16)[None, :]
        near_tally = near_tally + (near_places == picked).astype(jnp.bfloat16)
        hub_tally = hub_tally + (hub_places == picked).astype(jnp.bfloat16)
    near_tally, hub_tally = lax.optimization_barrier((near_tally, hub_tally))
    total = jnp.dot(hidden_one, near_tally, preferred_element_type=jnp.float32)
    total = total + jnp.dot(hub_table, hub_tally, preferred_element_type=jnp.float32)
    mean_two = (total / fanout).astype(jnp.bfloat16)
    own_cols = lax.dynamic_slice_in_dim(own_all, 0, tgt_dev, 1)
    near_cols = lax.dynamic_slice_in_dim(mean_all, 0, tgt_dev, 1)
    own_wide = jnp.maximum(
        left_product(self_one, own_cols) + left_product(neigh_one, near_cols), 0.0
    ).astype(jnp.bfloat16)
    mean_wide = lax.all_gather(mean_two, "feat", axis=0, tiled=True)
    v_own = lax.dynamic_slice_in_dim(self_two, column_index * hcols, hcols, 1)
    v_near = lax.dynamic_slice_in_dim(neigh_two, column_index * hcols, hcols, 1)
    result = left_product(v_own, own_wide) + left_product(v_near, mean_wide)
    return result.astype(jnp.bfloat16)


def solution(mesh):
    return jax.shard_map(
        body,
        mesh=mesh,
        in_specs=(
            P("feat", "dom"),
            P("dom", None, None),
            P(None, "dom", None),
            P(None, "dom"),
            P("dom", None),
            P("dom", None),
            P(),
            P(),
            P(),
            P(),
        ),
        out_specs=P("feat", "dom"),
        check_vma=False,
    )
```

```python
import math

import jax
import jax.numpy as jnp
from jax import lax
from jax.sharding import PartitionSpec as P


def left_product(weight, columns):
    return lax.dot_general(
        weight, columns, (((0,), (0,)), ((), ())), preferred_element_type=jnp.float32
    )


def pick_columns(data, index, groups=8):
    width, extent = data.shape
    span = extent // groups
    stacked = data.reshape(width, groups, span).transpose(1, 0, 2).reshape(groups * width, span)
    low = (index % span).astype(jnp.int16)
    high = index // span
    places = jnp.arange(span, dtype=jnp.int16)[:, None]
    onehot = (places == low[None, :]).astype(data.dtype)
    rows = jnp.dot(stacked, onehot, preferred_element_type=jnp.float32).astype(data.dtype)
    rows = rows.reshape(groups, width, index.shape[0])
    keep = high[None, None, :] == jnp.arange(groups, dtype=jnp.int32)[:, None, None]
    return jnp.sum(jnp.where(keep, rows, 0), axis=0, dtype=jnp.float32).astype(data.dtype)


def add_columns(values, index, weight, extent, groups=8):
    width, count = values.shape
    span = extent // groups
    values = jnp.concatenate([values, jnp.ones((1, count), values.dtype)], axis=0)
    values = values * weight.astype(values.dtype)[None, :]
    low = (index % span).astype(jnp.int16)
    high = index // span
    keep = high[None, None, :] == jnp.arange(groups, dtype=jnp.int32)[:, None, None]
    spread = jnp.where(keep, values[None], 0).astype(values.dtype).reshape(groups * (width + 1), count)
    places = jnp.arange(span, dtype=jnp.int16)[None, :]
    marks = (low[:, None] == places).astype(values.dtype)
    total = jnp.dot(spread, marks, preferred_element_type=jnp.float32)
    total = total.reshape(groups, width + 1, span).transpose(1, 0, 2).reshape(width + 1, extent)
    return (total[:width], total[width])


def body(
    features,
    edge_source,
    edge_target,
    edge_count,
    hub_local,
    second_source,
    self_one,
    neigh_one,
    self_two,
    neigh_two,
):
    n_feat = lax.axis_size("feat")
    n_dom = lax.axis_size("dom")
    column_index = lax.axis_index("feat")
    narrow, node_dev = features.shape
    sources = edge_source[0]
    slots = sources.shape[1]
    targets = edge_target[:, 0, :]
    counts = edge_count[:, 0]
    live = (jnp.arange(slots, dtype=jnp.int32)[None, :] < counts[:, None]).astype(jnp.float32)
    chosen = pick_columns(features, sources.reshape(-1)).reshape(narrow, n_dom, slots)
    received = lax.all_to_all(chosen, "dom", split_axis=1, concat_axis=1, tiled=True)
    neighbor_total, degree = add_columns(
        received.reshape(narrow, -1), targets.reshape(-1), live.reshape(-1), node_dev
    )
    mean_one = (neighbor_total / jnp.maximum(degree, 1.0)[None, :]).astype(jnp.bfloat16)
    hidden = self_one.shape[1]
    hcols = hidden // n_feat
    order = (column_index - jnp.arange(n_feat)) % n_feat

    def ring_gather(x):
        parts = [x]
        for shift in range(1, n_feat):
            pairs = [(j, (j + shift) % n_feat) for j in range(n_feat)]
            parts.append(lax.ppermute(x, "feat", perm=pairs))
        return jnp.concatenate(parts, axis=0)

    def ring_rows(weight):
        blocks = weight.reshape(n_feat, narrow, weight.shape[1])
        return jnp.take(blocks, order, axis=0).reshape(n_feat * narrow, weight.shape[1])

    self_one = ring_rows(self_one)
    neigh_one = ring_rows(neigh_one)
    own_all = ring_gather(features)
    mean_all = ring_gather(mean_one)
    w_own = lax.dynamic_slice_in_dim(self_one, column_index * hcols, hcols, 1)
    w_near = lax.dynamic_slice_in_dim(neigh_one, column_index * hcols, hcols, 1)
    pre_one = left_product(w_own, own_all) + left_product(w_near, mean_all)
    hidden_one = jnp.maximum(pre_one, 0.0).astype(jnp.bfloat16)
    hub_rows = hidden_one[:, hub_local[0]]
    hub_count = hub_rows.shape[1]
    spread = jnp.broadcast_to(hub_rows[None], (n_dom,) + hub_rows.shape)
    landed = lax.all_to_all(spread, "dom", split_axis=0, concat_axis=0, tiled=True)
    hub_table = landed.transpose(1, 0, 2).reshape(hidden_one.shape[0], n_dom * hub_count)
    tgt_dev, fanout = second_source.shape
    near_places = jnp.arange(node_dev, dtype=jnp.int16)[:, None]
    hub_places = (node_dev + jnp.arange(n_dom * hub_count, dtype=jnp.int32)).astype(jnp.int16)[:, None]
    near_tally = jnp.zeros((node_dev, tgt_dev), jnp.bfloat16)
    hub_tally = jnp.zeros((n_dom * hub_count, tgt_dev), jnp.bfloat16)
    for column in range(fanout):
        picked = second_source[:, column].astype(jnp.int16)[None, :]
        near_tally = near_tally + (near_places == picked).astype(jnp.bfloat16)
        hub_tally = hub_tally + (hub_places == picked).astype(jnp.bfloat16)
    near_tally, hub_tally = lax.optimization_barrier((near_tally, hub_tally))
    total = jnp.dot(hidden_one, near_tally, preferred_element_type=jnp.float32)
    total = total + jnp.dot(hub_table, hub_tally, preferred_element_type=jnp.float32)
    mean_two = (total / fanout).astype(jnp.bfloat16)
    own_cols = lax.dynamic_slice_in_dim(own_all, 0, tgt_dev, 1)
    near_cols = lax.dynamic_slice_in_dim(mean_all, 0, tgt_dev, 1)
    own_wide = jnp.maximum(
        left_product(self_one, own_cols) + left_product(neigh_one, near_cols), 0.0
    ).astype(jnp.bfloat16)
    mean_wide = lax.all_gather(mean_two, "feat", axis=0, tiled=True)
    v_own = lax.dynamic_slice_in_dim(self_two, column_index * hcols, hcols, 1)
    v_near = lax.dynamic_slice_in_dim(neigh_two, column_index * hcols, hcols, 1)
    result = left_product(v_own, own_wide) + left_product(v_near, mean_wide)
    return result.astype(jnp.bfloat16)


def solution(mesh):
    return jax.shard_map(
        body,
        mesh=mesh,
        in_specs=(
            P("feat", "dom"),
            P("dom", None, None),
            P(None, "dom", None),
            P(None, "dom"),
            P("dom", None),
            P("dom", None),
            P(),
            P(),
            P(),
            P(),
        ),
        out_specs=P("feat", "dom"),
        check_vma=False,
    )
```

```python
import math

import jax
import jax.numpy as jnp
from jax import lax
from jax.sharding import PartitionSpec as P


def left_product(weight, columns):
    return lax.dot_general(
        weight, columns, (((0,), (0,)), ((), ())), preferred_element_type=jnp.float32
    )


def pick_columns(data, index, groups=8):
    width, extent = data.shape
    span = extent // groups
    stacked = data.reshape(width, groups, span).transpose(1, 0, 2).reshape(groups * width, span)
    low = (index % span).astype(jnp.int16)
    high = index // span
    places = jnp.arange(span, dtype=jnp.int16)[:, None]
    onehot = (places == low[None, :]).astype(data.dtype)
    rows = jnp.dot(stacked, onehot, preferred_element_type=jnp.float32).astype(data.dtype)
    rows = rows.reshape(groups, width, index.shape[0])
    keep = high[None, None, :] == jnp.arange(groups, dtype=jnp.int32)[:, None, None]
    return jnp.sum(jnp.where(keep, rows, 0), axis=0, dtype=jnp.float32).astype(data.dtype)


def add_columns(values, index, weight, extent, groups=8):
    width, count = values.shape
    span = extent // groups
    values = jnp.concatenate([values, jnp.ones((1, count), values.dtype)], axis=0)
    values = values * weight.astype(values.dtype)[None, :]
    low = (index % span).astype(jnp.int16)
    high = index // span
    keep = high[None, None, :] == jnp.arange(groups, dtype=jnp.int32)[:, None, None]
    spread = jnp.where(keep, values[None], 0).astype(values.dtype).reshape(groups * (width + 1), count)
    places = jnp.arange(span, dtype=jnp.int16)[None, :]
    marks = (low[:, None] == places).astype(values.dtype)
    total = jnp.dot(spread, marks, preferred_element_type=jnp.float32)
    total = total.reshape(groups, width + 1, span).transpose(1, 0, 2).reshape(width + 1, extent)
    return (total[:width], total[width])


def body(
    features,
    edge_source,
    edge_target,
    edge_count,
    hub_local,
    second_source,
    self_one,
    neigh_one,
    self_two,
    neigh_two,
):
    n_feat = lax.axis_size("feat")
    n_dom = lax.axis_size("dom")
    column_index = lax.axis_index("feat")
    narrow, node_dev = features.shape
    sources = edge_source[0]
    slots = sources.shape[1]
    targets = edge_target[:, 0, :]
    counts = edge_count[:, 0]
    live = (jnp.arange(slots, dtype=jnp.int32)[None, :] < counts[:, None]).astype(jnp.float32)
    chosen = pick_columns(features, sources.reshape(-1)).reshape(narrow, n_dom, slots)
    received = lax.all_to_all(chosen, "dom", split_axis=1, concat_axis=1, tiled=True)
    neighbor_total, degree = add_columns(
        received.reshape(narrow, -1), targets.reshape(-1), live.reshape(-1), node_dev
    )
    mean_one = (neighbor_total / jnp.maximum(degree, 1.0)[None, :]).astype(jnp.bfloat16)
    late_source, mean_one = lax.optimization_barrier((second_source, mean_one))
    hidden = self_one.shape[1]
    hcols = hidden // n_feat
    order = (column_index - jnp.arange(n_feat)) % n_feat

    def ring_gather(x):
        parts = [x]
        for shift in range(1, n_feat):
            pairs = [(j, (j + shift) % n_feat) for j in range(n_feat)]
            parts.append(lax.ppermute(x, "feat", perm=pairs))
        return jnp.concatenate(parts, axis=0)

    def ring_rows(weight):
        blocks = weight.reshape(n_feat, narrow, weight.shape[1])
        return jnp.take(blocks, order, axis=0).reshape(n_feat * narrow, weight.shape[1])

    self_one = ring_rows(self_one)
    neigh_one = ring_rows(neigh_one)
    own_all = ring_gather(features)
    mean_all = ring_gather(mean_one)
    w_own = lax.dynamic_slice_in_dim(self_one, column_index * hcols, hcols, 1)
    w_near = lax.dynamic_slice_in_dim(neigh_one, column_index * hcols, hcols, 1)
    pre_one = left_product(w_own, own_all) + left_product(w_near, mean_all)
    hidden_one = jnp.maximum(pre_one, 0.0).astype(jnp.bfloat16)
    hub_rows = hidden_one[:, hub_local[0]]
    hub_count = hub_rows.shape[1]
    spread = jnp.broadcast_to(hub_rows[None], (n_dom,) + hub_rows.shape)
    landed = lax.all_to_all(spread, "dom", split_axis=0, concat_axis=0, tiled=True)
    hub_table = landed.transpose(1, 0, 2).reshape(hidden_one.shape[0], n_dom * hub_count)
    tgt_dev, fanout = second_source.shape
    near_places = jnp.arange(node_dev, dtype=jnp.int16)[:, None]
    hub_places = (node_dev + jnp.arange(n_dom * hub_count, dtype=jnp.int32)).astype(jnp.int16)[:, None]
    near_tally = jnp.zeros((node_dev, tgt_dev), jnp.bfloat16)
    hub_tally = jnp.zeros((n_dom * hub_count, tgt_dev), jnp.bfloat16)
    for column in range(fanout):
        picked = second_source[:, column].astype(jnp.int16)[None, :]
        near_tally = near_tally + (near_places == picked).astype(jnp.bfloat16)
        late = late_source[:, column].astype(jnp.int16)[None, :]
        hub_tally = hub_tally + (hub_places == late).astype(jnp.bfloat16)
    near_tally = lax.optimization_barrier(near_tally)
    hub_tally = lax.optimization_barrier(hub_tally)
    total = jnp.dot(hidden_one, near_tally, preferred_element_type=jnp.float32)
    total = total + jnp.dot(hub_table, hub_tally, preferred_element_type=jnp.float32)
    mean_two = (total / fanout).astype(jnp.bfloat16)
    own_cols = lax.dynamic_slice_in_dim(own_all, 0, tgt_dev, 1)
    near_cols = lax.dynamic_slice_in_dim(mean_all, 0, tgt_dev, 1)
    own_wide = jnp.maximum(
        left_product(self_one, own_cols) + left_product(neigh_one, near_cols), 0.0
    ).astype(jnp.bfloat16)
    mean_wide = ring_gather(mean_two)
    v_own = lax.dynamic_slice_in_dim(self_two, column_index * hcols, hcols, 1)
    v_near = lax.dynamic_slice_in_dim(neigh_two, column_index * hcols, hcols, 1)
    v_near = jnp.take(v_near.reshape(n_feat, hidden // n_feat, hcols), order, axis=0).reshape(hidden, hcols)
    result = left_product(v_own, own_wide) + left_product(v_near, mean_wide)
    return result.astype(jnp.bfloat16)


def solution(mesh):
    return jax.shard_map(
        body,
        mesh=mesh,
        in_specs=(
            P("feat", "dom"),
            P("dom", None, None),
            P(None, "dom", None),
            P(None, "dom"),
            P("dom", None),
            P("dom", None),
            P(),
            P(),
            P(),
            P(),
        ),
        out_specs=P("feat", "dom"),
        check_vma=False,
    )
```

```python
import math

import jax
import jax.numpy as jnp
from jax import lax
from jax.sharding import PartitionSpec as P


def left_product(weight, columns):
    return lax.dot_general(
        weight, columns, (((0,), (0,)), ((), ())), preferred_element_type=jnp.float32
    )


def pick_columns(data, index, groups=8):
    width, extent = data.shape
    span = extent // groups
    stacked = data.reshape(width, groups, span).transpose(1, 0, 2).reshape(groups * width, span)
    low = (index % span).astype(jnp.int16)
    high = index // span
    places = jnp.arange(span, dtype=jnp.int16)[:, None]
    onehot = (places == low[None, :]).astype(data.dtype)
    rows = jnp.dot(stacked, onehot, preferred_element_type=jnp.float32).astype(data.dtype)
    rows = rows.reshape(groups, width, index.shape[0])
    keep = high[None, None, :] == jnp.arange(groups, dtype=jnp.int32)[:, None, None]
    return jnp.sum(jnp.where(keep, rows, 0), axis=0, dtype=jnp.float32).astype(data.dtype)


def add_columns(values, index, weight, extent, groups=8):
    width, count = values.shape
    span = extent // groups
    values = jnp.concatenate([values, jnp.ones((1, count), values.dtype)], axis=0)
    values = values * weight.astype(values.dtype)[None, :]
    low = (index % span).astype(jnp.int16)
    high = index // span
    keep = high[None, None, :] == jnp.arange(groups, dtype=jnp.int32)[:, None, None]
    spread = jnp.where(keep, values[None], 0).astype(values.dtype).reshape(groups * (width + 1), count)
    places = jnp.arange(span, dtype=jnp.int16)[None, :]
    marks = (low[:, None] == places).astype(values.dtype)
    total = jnp.dot(spread, marks, preferred_element_type=jnp.float32)
    total = total.reshape(groups, width + 1, span).transpose(1, 0, 2).reshape(width + 1, extent)
    return (total[:width], total[width])


def body(
    features,
    edge_source,
    edge_target,
    edge_count,
    hub_local,
    second_source,
    self_one,
    neigh_one,
    self_two,
    neigh_two,
):
    n_feat = lax.axis_size("feat")
    n_dom = lax.axis_size("dom")
    column_index = lax.axis_index("feat")
    narrow, node_dev = features.shape
    sources = edge_source[0]
    slots = sources.shape[1]
    targets = edge_target[:, 0, :]
    counts = edge_count[:, 0]
    live = (jnp.arange(slots, dtype=jnp.int32)[None, :] < counts[:, None]).astype(jnp.float32)
    chosen = pick_columns(features, sources.reshape(-1)).reshape(narrow, n_dom, slots)
    received = lax.all_to_all(chosen, "dom", split_axis=1, concat_axis=1, tiled=True)
    neighbor_total, degree = add_columns(
        received.reshape(narrow, -1), targets.reshape(-1), live.reshape(-1), node_dev
    )
    mean_one = (neighbor_total / jnp.maximum(degree, 1.0)[None, :]).astype(jnp.bfloat16)
    late_source, mean_one = lax.optimization_barrier((second_source, mean_one))
    hidden = self_one.shape[1]
    hcols = hidden // n_feat
    order = (column_index - jnp.arange(n_feat)) % n_feat

    def ring_gather(x):
        parts = [x]
        for shift in range(1, n_feat):
            pairs = [(j, (j + shift) % n_feat) for j in range(n_feat)]
            parts.append(lax.ppermute(x, "feat", perm=pairs))
        return jnp.concatenate(parts, axis=0)

    def ring_rows(weight):
        blocks = weight.reshape(n_feat, narrow, weight.shape[1])
        return jnp.take(blocks, order, axis=0).reshape(n_feat * narrow, weight.shape[1])

    hub_index = hub_local[0]
    hub_count = hub_index.shape[0]
    hub_in = jnp.concatenate([features[:, hub_index], mean_one[:, hub_index]], axis=0)
    n_all = n_dom * n_feat
    spread = jnp.broadcast_to(hub_in[None], (n_all,) + hub_in.shape)
    landed = lax.all_to_all(spread, ("dom", "feat"), split_axis=0, concat_axis=0, tiled=True)
    landed = landed.reshape(n_dom, n_feat, 2, narrow, hub_count)
    hub_feat = landed[:, :, 0].transpose(1, 2, 0, 3).reshape(n_feat * narrow, n_dom * hub_count)
    hub_mean = landed[:, :, 1].transpose(1, 2, 0, 3).reshape(n_feat * narrow, n_dom * hub_count)
    u_own = lax.dynamic_slice_in_dim(self_one, column_index * hcols, hcols, 1)
    u_near = lax.dynamic_slice_in_dim(neigh_one, column_index * hcols, hcols, 1)
    hub_table = jnp.maximum(
        left_product(u_own, hub_feat) + left_product(u_near, hub_mean), 0.0
    ).astype(jnp.bfloat16)
    self_one = ring_rows(self_one)
    neigh_one = ring_rows(neigh_one)
    own_all = ring_gather(features)
    mean_all = ring_gather(mean_one)
    w_own = lax.dynamic_slice_in_dim(self_one, column_index * hcols, hcols, 1)
    w_near = lax.dynamic_slice_in_dim(neigh_one, column_index * hcols, hcols, 1)
    pre_one = left_product(w_own, own_all) + left_product(w_near, mean_all)
    hidden_one = jnp.maximum(pre_one, 0.0).astype(jnp.bfloat16)
    tgt_dev, fanout = second_source.shape
    near_places = jnp.arange(node_dev, dtype=jnp.int16)[:, None]
    hub_places = (node_dev + jnp.arange(n_dom * hub_count, dtype=jnp.int32)).astype(jnp.int16)[:, None]
    near_tally = jnp.zeros((node_dev, tgt_dev), jnp.bfloat16)
    hub_tally = jnp.zeros((n_dom * hub_count, tgt_dev), jnp.bfloat16)
    for column in range(fanout):
        picked = second_source[:, column].astype(jnp.int16)[None, :]
        near_tally = near_tally + (near_places == picked).astype(jnp.bfloat16)
        late = late_source[:, column].astype(jnp.int16)[None, :]
        hub_tally = hub_tally + (hub_places == late).astype(jnp.bfloat16)
    near_tally = lax.optimization_barrier(near_tally)
    hub_tally = lax.optimization_barrier(hub_tally)
    total = jnp.dot(hidden_one, near_tally, preferred_element_type=jnp.float32)
    total = total + jnp.dot(hub_table, hub_tally, preferred_element_type=jnp.float32)
    mean_two = (total / fanout).astype(jnp.bfloat16)
    own_cols = lax.dynamic_slice_in_dim(own_all, 0, tgt_dev, 1)
    near_cols = lax.dynamic_slice_in_dim(mean_all, 0, tgt_dev, 1)
    own_wide = jnp.maximum(
        left_product(self_one, own_cols) + left_product(neigh_one, near_cols), 0.0
    ).astype(jnp.bfloat16)
    mean_wide = ring_gather(mean_two)
    v_own = lax.dynamic_slice_in_dim(self_two, column_index * hcols, hcols, 1)
    v_near = lax.dynamic_slice_in_dim(neigh_two, column_index * hcols, hcols, 1)
    v_near = jnp.take(v_near.reshape(n_feat, hidden // n_feat, hcols), order, axis=0).reshape(hidden, hcols)
    result = left_product(v_own, own_wide) + left_product(v_near, mean_wide)
    return result.astype(jnp.bfloat16)


def solution(mesh):
    return jax.shard_map(
        body,
        mesh=mesh,
        in_specs=(
            P("feat", "dom"),
            P("dom", None, None),
            P(None, "dom", None),
            P(None, "dom"),
            P("dom", None),
            P("dom", None),
            P(),
            P(),
            P(),
            P(),
        ),
        out_specs=P("feat", "dom"),
        check_vma=False,
    )
```

```python
import math

import jax
import jax.numpy as jnp
from jax import lax
from jax.sharding import PartitionSpec as P


def left_product(weight, columns):
    return lax.dot_general(
        weight, columns, (((0,), (0,)), ((), ())), preferred_element_type=jnp.float32
    )


def pick_columns(data, index, groups=8):
    width, extent = data.shape
    span = extent // groups
    stacked = data.reshape(width, groups, span).transpose(1, 0, 2).reshape(groups * width, span)
    low = (index % span).astype(jnp.int16)
    high = index // span
    places = jnp.arange(span, dtype=jnp.int16)[:, None]
    onehot = (places == low[None, :]).astype(data.dtype)
    rows = jnp.dot(stacked, onehot, preferred_element_type=jnp.float32).astype(data.dtype)
    rows = rows.reshape(groups, width, index.shape[0])
    keep = high[None, None, :] == jnp.arange(groups, dtype=jnp.int32)[:, None, None]
    return jnp.sum(jnp.where(keep, rows, 0), axis=0, dtype=jnp.float32).astype(data.dtype)


def add_columns(values, index, weight, extent, groups=8):
    width, count = values.shape
    span = extent // groups
    values = jnp.concatenate([values, jnp.ones((1, count), values.dtype)], axis=0)
    values = values * weight.astype(values.dtype)[None, :]
    low = (index % span).astype(jnp.int16)
    high = index // span
    keep = high[None, None, :] == jnp.arange(groups, dtype=jnp.int32)[:, None, None]
    spread = jnp.where(keep, values[None], 0).astype(values.dtype).reshape(groups * (width + 1), count)
    places = jnp.arange(span, dtype=jnp.int16)[None, :]
    marks = (low[:, None] == places).astype(values.dtype)
    total = jnp.dot(spread, marks, preferred_element_type=jnp.float32)
    total = total.reshape(groups, width + 1, span).transpose(1, 0, 2).reshape(width + 1, extent)
    return (total[:width], total[width])


def body(
    features,
    edge_source,
    edge_target,
    edge_count,
    hub_local,
    second_source,
    self_one,
    neigh_one,
    self_two,
    neigh_two,
):
    n_feat = lax.axis_size("feat")
    n_dom = lax.axis_size("dom")
    column_index = lax.axis_index("feat")
    narrow, node_dev = features.shape
    sources = edge_source[0]
    slots = sources.shape[1]
    targets = edge_target[:, 0, :]
    counts = edge_count[:, 0]
    live = (jnp.arange(slots, dtype=jnp.int32)[None, :] < counts[:, None]).astype(jnp.float32)
    chosen = pick_columns(features, sources.reshape(-1)).reshape(narrow, n_dom, slots)
    received = lax.all_to_all(chosen, "dom", split_axis=1, concat_axis=1, tiled=True)
    neighbor_total, degree = add_columns(
        received.reshape(narrow, -1), targets.reshape(-1), live.reshape(-1), node_dev
    )
    mean_one = (neighbor_total / jnp.maximum(degree, 1.0)[None, :]).astype(jnp.bfloat16)
    late_source, mean_one = lax.optimization_barrier((second_source, mean_one))
    hidden = self_one.shape[1]
    hcols = hidden // n_feat
    order = (column_index - jnp.arange(n_feat)) % n_feat

    def ring_gather(x):
        parts = [x]
        for shift in range(1, n_feat):
            pairs = [(j, (j + shift) % n_feat) for j in range(n_feat)]
            parts.append(lax.ppermute(x, "feat", perm=pairs))
        return jnp.concatenate(parts, axis=0)

    def ring_rows(weight):
        blocks = weight.reshape(n_feat, narrow, weight.shape[1])
        return jnp.take(blocks, order, axis=0).reshape(n_feat * narrow, weight.shape[1])

    self_one = ring_rows(self_one)
    neigh_one = ring_rows(neigh_one)
    own_all = ring_gather(features)
    mean_all = ring_gather(mean_one)
    w_own = lax.dynamic_slice_in_dim(self_one, column_index * hcols, hcols, 1)
    w_near = lax.dynamic_slice_in_dim(neigh_one, column_index * hcols, hcols, 1)
    pre_one = left_product(w_own, own_all) + left_product(w_near, mean_all)
    hidden_one = jnp.maximum(pre_one, 0.0).astype(jnp.bfloat16)
    hub_marks = (jnp.arange(node_dev, dtype=jnp.int32)[:, None] == hub_local[0][None, :]).astype(jnp.bfloat16)
    hub_rows = jnp.dot(hidden_one, hub_marks, preferred_element_type=jnp.float32).astype(jnp.bfloat16)
    hub_count = hub_rows.shape[1]
    spread = jnp.broadcast_to(hub_rows[None], (n_dom,) + hub_rows.shape)
    landed = lax.all_to_all(spread, "dom", split_axis=0, concat_axis=0, tiled=True)
    hub_table = landed.transpose(1, 0, 2).reshape(hidden_one.shape[0], n_dom * hub_count)
    tgt_dev, fanout = second_source.shape
    near_places = jnp.arange(node_dev, dtype=jnp.int16)[:, None]
    hub_places = (node_dev + jnp.arange(n_dom * hub_count, dtype=jnp.int32)).astype(jnp.int16)[:, None]
    near_tally = jnp.zeros((node_dev, tgt_dev), jnp.bfloat16)
    hub_tally = jnp.zeros((n_dom * hub_count, tgt_dev), jnp.bfloat16)
    for column in range(fanout):
        picked = second_source[:, column].astype(jnp.int16)[None, :]
        near_tally = near_tally + (near_places == picked).astype(jnp.bfloat16)
        late = late_source[:, column].astype(jnp.int16)[None, :]
        hub_tally = hub_tally + (hub_places == late).astype(jnp.bfloat16)
    near_tally = lax.optimization_barrier(near_tally)
    hub_tally = lax.optimization_barrier(hub_tally)
    total = jnp.dot(hidden_one, near_tally, preferred_element_type=jnp.float32)
    total = total + jnp.dot(hub_table, hub_tally, preferred_element_type=jnp.float32)
    mean_two = (total / fanout).astype(jnp.bfloat16)
    own_cols = lax.dynamic_slice_in_dim(own_all, 0, tgt_dev, 1)
    near_cols = lax.dynamic_slice_in_dim(mean_all, 0, tgt_dev, 1)
    own_wide = jnp.maximum(
        left_product(self_one, own_cols) + left_product(neigh_one, near_cols), 0.0
    ).astype(jnp.bfloat16)
    mean_wide = ring_gather(mean_two)
    v_own = lax.dynamic_slice_in_dim(self_two, column_index * hcols, hcols, 1)
    v_near = lax.dynamic_slice_in_dim(neigh_two, column_index * hcols, hcols, 1)
    v_near = jnp.take(v_near.reshape(n_feat, hidden // n_feat, hcols), order, axis=0).reshape(hidden, hcols)
    result = left_product(v_own, own_wide) + left_product(v_near, mean_wide)
    return result.astype(jnp.bfloat16)


def solution(mesh):
    return jax.shard_map(
        body,
        mesh=mesh,
        in_specs=(
            P("feat", "dom"),
            P("dom", None, None),
            P(None, "dom", None),
            P(None, "dom"),
            P("dom", None),
            P("dom", None),
            P(),
            P(),
            P(),
            P(),
        ),
        out_specs=P("feat", "dom"),
        check_vma=False,
    )
```

```python
import math

import jax
import jax.numpy as jnp
from jax import lax
from jax.sharding import PartitionSpec as P


def left_product(weight, columns):
    return lax.dot_general(
        weight, columns, (((0,), (0,)), ((), ())), preferred_element_type=jnp.float32
    )


def pick_columns(data, index, groups=8):
    width, extent = data.shape
    span = extent // groups
    stacked = data.reshape(width, groups, span).transpose(1, 0, 2).reshape(groups * width, span)
    low = (index % span).astype(jnp.int16)
    high = index // span
    places = jnp.arange(span, dtype=jnp.int16)[:, None]
    onehot = (places == low[None, :]).astype(data.dtype)
    rows = jnp.dot(stacked, onehot, preferred_element_type=jnp.float32).astype(data.dtype)
    rows = rows.reshape(groups, width, index.shape[0])
    keep = high[None, None, :] == jnp.arange(groups, dtype=jnp.int32)[:, None, None]
    return jnp.sum(jnp.where(keep, rows, 0), axis=0, dtype=jnp.float32).astype(data.dtype)


def add_columns(values, index, weight, extent, groups=8):
    width, count = values.shape
    span = extent // groups
    values = jnp.concatenate([values, jnp.ones((1, count), values.dtype)], axis=0)
    values = values * weight.astype(values.dtype)[None, :]
    low = (index % span).astype(jnp.int16)
    high = index // span
    keep = high[None, None, :] == jnp.arange(groups, dtype=jnp.int32)[:, None, None]
    spread = jnp.where(keep, values[None], 0).astype(values.dtype).reshape(groups * (width + 1), count)
    places = jnp.arange(span, dtype=jnp.int16)[None, :]
    marks = (low[:, None] == places).astype(values.dtype)
    total = jnp.dot(spread, marks, preferred_element_type=jnp.float32)
    total = total.reshape(groups, width + 1, span).transpose(1, 0, 2).reshape(width + 1, extent)
    return (total[:width], total[width])


def body(
    features,
    edge_source,
    edge_target,
    edge_count,
    hub_local,
    second_source,
    self_one,
    neigh_one,
    self_two,
    neigh_two,
):
    n_feat = lax.axis_size("feat")
    n_dom = lax.axis_size("dom")
    column_index = lax.axis_index("feat")
    narrow, node_dev = features.shape
    sources = edge_source[0]
    slots = sources.shape[1]
    targets = edge_target[:, 0, :]
    counts = edge_count[:, 0]
    live = (jnp.arange(slots, dtype=jnp.int32)[None, :] < counts[:, None]).astype(jnp.float32)
    chosen = pick_columns(features, sources.reshape(-1)).reshape(narrow, n_dom, slots)
    received = lax.all_to_all(chosen, "dom", split_axis=1, concat_axis=1, tiled=True)
    neighbor_total, degree = add_columns(
        received.reshape(narrow, -1), targets.reshape(-1), live.reshape(-1), node_dev
    )
    mean_one = (neighbor_total / jnp.maximum(degree, 1.0)[None, :]).astype(jnp.bfloat16)
    late_source, mean_one = lax.optimization_barrier((second_source, mean_one))
    hidden = self_one.shape[1]
    hcols = hidden // n_feat
    order = (column_index - jnp.arange(n_feat)) % n_feat

    def ring_gather(x):
        parts = [x]
        for shift in range(1, n_feat):
            pairs = [(j, (j + shift) % n_feat) for j in range(n_feat)]
            parts.append(lax.ppermute(x, "feat", perm=pairs))
        return jnp.concatenate(parts, axis=0)

    def ring_rows(weight):
        blocks = weight.reshape(n_feat, narrow, weight.shape[1])
        return jnp.take(blocks, order, axis=0).reshape(n_feat * narrow, weight.shape[1])

    self_one = ring_rows(self_one)
    neigh_one = ring_rows(neigh_one)
    own_all = ring_gather(features)
    mean_all = ring_gather(mean_one)
    w_own = lax.dynamic_slice_in_dim(self_one, column_index * hcols, hcols, 1)
    w_near = lax.dynamic_slice_in_dim(neigh_one, column_index * hcols, hcols, 1)
    pre_one = left_product(w_own, own_all) + left_product(w_near, mean_all)
    hidden_one = jnp.maximum(pre_one, 0.0).astype(jnp.bfloat16)
    hub_marks = (jnp.arange(node_dev, dtype=jnp.int32)[:, None] == hub_local[0][None, :]).astype(jnp.bfloat16)
    hub_own = jnp.dot(own_all, hub_marks, preferred_element_type=jnp.float32).astype(jnp.bfloat16)
    hub_near = jnp.dot(mean_all, hub_marks, preferred_element_type=jnp.float32).astype(jnp.bfloat16)
    hub_rows = jnp.maximum(
        left_product(w_own, hub_own) + left_product(w_near, hub_near), 0.0
    ).astype(jnp.bfloat16)
    hub_count = hub_rows.shape[1]
    spread = jnp.broadcast_to(hub_rows[None], (n_dom,) + hub_rows.shape)
    landed = lax.all_to_all(spread, "dom", split_axis=0, concat_axis=0, tiled=True)
    hub_table = landed.transpose(1, 0, 2).reshape(hidden_one.shape[0], n_dom * hub_count)
    tgt_dev, fanout = second_source.shape
    near_places = jnp.arange(node_dev, dtype=jnp.int16)[:, None]
    hub_places = (node_dev + jnp.arange(n_dom * hub_count, dtype=jnp.int32)).astype(jnp.int16)[:, None]
    near_tally = jnp.zeros((node_dev, tgt_dev), jnp.bfloat16)
    hub_tally = jnp.zeros((n_dom * hub_count, tgt_dev), jnp.bfloat16)
    for column in range(fanout):
        picked = second_source[:, column].astype(jnp.int16)[None, :]
        near_tally = near_tally + (near_places == picked).astype(jnp.bfloat16)
        late = late_source[:, column].astype(jnp.int16)[None, :]
        hub_tally = hub_tally + (hub_places == late).astype(jnp.bfloat16)
    near_tally = lax.optimization_barrier(near_tally)
    hub_tally = lax.optimization_barrier(hub_tally)
    total = jnp.dot(hidden_one, near_tally, preferred_element_type=jnp.float32)
    total = total + jnp.dot(hub_table, hub_tally, preferred_element_type=jnp.float32)
    mean_two = (total / fanout).astype(jnp.bfloat16)
    own_cols = lax.dynamic_slice_in_dim(own_all, 0, tgt_dev, 1)
    near_cols = lax.dynamic_slice_in_dim(mean_all, 0, tgt_dev, 1)
    own_wide = jnp.maximum(
        left_product(self_one, own_cols) + left_product(neigh_one, near_cols), 0.0
    ).astype(jnp.bfloat16)
    mean_wide = ring_gather(mean_two)
    v_own = lax.dynamic_slice_in_dim(self_two, column_index * hcols, hcols, 1)
    v_near = lax.dynamic_slice_in_dim(neigh_two, column_index * hcols, hcols, 1)
    v_near = jnp.take(v_near.reshape(n_feat, hidden // n_feat, hcols), order, axis=0).reshape(hidden, hcols)
    result = left_product(v_own, own_wide) + left_product(v_near, mean_wide)
    return result.astype(jnp.bfloat16)


def solution(mesh):
    return jax.shard_map(
        body,
        mesh=mesh,
        in_specs=(
            P("feat", "dom"),
            P("dom", None, None),
            P(None, "dom", None),
            P(None, "dom"),
            P("dom", None),
            P("dom", None),
            P(),
            P(),
            P(),
            P(),
        ),
        out_specs=P("feat", "dom"),
        check_vma=False,
    )
```

```python
import math

import jax
import jax.numpy as jnp
from jax import lax
from jax.sharding import PartitionSpec as P


def left_product(weight, columns):
    return lax.dot_general(
        weight, columns, (((0,), (0,)), ((), ())), preferred_element_type=jnp.float32
    )


def pick_columns(data, index, groups=8):
    width, extent = data.shape
    span = extent // groups
    stacked = data.reshape(width, groups, span).transpose(1, 0, 2).reshape(groups * width, span)
    low = (index % span).astype(jnp.int16)
    high = index // span
    places = jnp.arange(span, dtype=jnp.int16)[:, None]
    onehot = (places == low[None, :]).astype(data.dtype)
    rows = jnp.dot(stacked, onehot, preferred_element_type=jnp.float32).astype(data.dtype)
    rows = rows.reshape(groups, width, index.shape[0])
    keep = high[None, None, :] == jnp.arange(groups, dtype=jnp.int32)[:, None, None]
    return jnp.sum(jnp.where(keep, rows, 0), axis=0, dtype=jnp.float32).astype(data.dtype)


def add_columns(values, index, weight, extent, groups=8):
    width, count = values.shape
    span = extent // groups
    values = jnp.concatenate([values, jnp.ones((1, count), values.dtype)], axis=0)
    values = values * weight.astype(values.dtype)[None, :]
    low = (index % span).astype(jnp.int16)
    high = index // span
    keep = high[None, None, :] == jnp.arange(groups, dtype=jnp.int32)[:, None, None]
    spread = jnp.where(keep, values[None], 0).astype(values.dtype).reshape(groups * (width + 1), count)
    places = jnp.arange(span, dtype=jnp.int16)[None, :]
    marks = (low[:, None] == places).astype(values.dtype)
    total = jnp.dot(spread, marks, preferred_element_type=jnp.float32)
    total = total.reshape(groups, width + 1, span).transpose(1, 0, 2).reshape(width + 1, extent)
    return (total[:width], total[width])


def body(
    features,
    edge_source,
    edge_target,
    edge_count,
    hub_local,
    second_source,
    self_one,
    neigh_one,
    self_two,
    neigh_two,
):
    n_feat = lax.axis_size("feat")
    n_dom = lax.axis_size("dom")
    column_index = lax.axis_index("feat")
    narrow, node_dev = features.shape
    sources = edge_source[0]
    slots = sources.shape[1]
    targets = edge_target[:, 0, :]
    counts = edge_count[:, 0]
    live = (jnp.arange(slots, dtype=jnp.int32)[None, :] < counts[:, None]).astype(jnp.float32)
    chosen = pick_columns(features, sources.reshape(-1)).reshape(narrow, n_dom, slots)
    received = lax.all_to_all(chosen, "dom", split_axis=1, concat_axis=1, tiled=True)
    neighbor_total, degree = add_columns(
        received.reshape(narrow, -1), targets.reshape(-1), live.reshape(-1), node_dev
    )
    mean_one = (neighbor_total / jnp.maximum(degree, 1.0)[None, :]).astype(jnp.bfloat16)
    late_source, mean_one = lax.optimization_barrier((second_source, mean_one))
    hidden = self_one.shape[1]
    hcols = hidden // n_feat
    order = (column_index - jnp.arange(n_feat)) % n_feat

    def ring_gather(x):
        parts = [x]
        for shift in range(1, n_feat):
            pairs = [(j, (j + shift) % n_feat) for j in range(n_feat)]
            parts.append(lax.ppermute(x, "feat", perm=pairs))
        return jnp.concatenate(parts, axis=0)

    def ring_rows(weight):
        blocks = weight.reshape(n_feat, narrow, weight.shape[1])
        return jnp.take(blocks, order, axis=0).reshape(n_feat * narrow, weight.shape[1])

    self_one = ring_rows(self_one)
    neigh_one = ring_rows(neigh_one)
    half = lax.ppermute(features, "feat", perm=[(j, (j + 1) % n_feat) for j in range(n_feat)])
    pair = jnp.concatenate([features, half], axis=0)
    far = lax.ppermute(pair, "feat", perm=[(j, (j + 2) % n_feat) for j in range(n_feat)])
    own_all = jnp.concatenate([pair, far], axis=0)
    mean_all = ring_gather(mean_one)
    w_own = lax.dynamic_slice_in_dim(self_one, column_index * hcols, hcols, 1)
    w_near = lax.dynamic_slice_in_dim(neigh_one, column_index * hcols, hcols, 1)
    pre_one = left_product(w_own, own_all) + left_product(w_near, mean_all)
    hidden_one = jnp.maximum(pre_one, 0.0).astype(jnp.bfloat16)
    hub_marks = (jnp.arange(node_dev, dtype=jnp.int32)[:, None] == hub_local[0][None, :]).astype(jnp.bfloat16)
    hub_rows = jnp.dot(hidden_one, hub_marks, preferred_element_type=jnp.float32).astype(jnp.bfloat16)
    hub_count = hub_rows.shape[1]
    spread = jnp.broadcast_to(hub_rows[None], (n_dom,) + hub_rows.shape)
    landed = lax.all_to_all(spread, "dom", split_axis=0, concat_axis=0, tiled=True)
    hub_table = landed.transpose(1, 0, 2).reshape(hidden_one.shape[0], n_dom * hub_count)
    tgt_dev, fanout = second_source.shape
    near_places = jnp.arange(node_dev, dtype=jnp.int16)[:, None]
    hub_places = (node_dev + jnp.arange(n_dom * hub_count, dtype=jnp.int32)).astype(jnp.int16)[:, None]
    near_tally = jnp.zeros((node_dev, tgt_dev), jnp.bfloat16)
    hub_tally = jnp.zeros((n_dom * hub_count, tgt_dev), jnp.bfloat16)
    for column in range(fanout):
        picked = second_source[:, column].astype(jnp.int16)[None, :]
        near_tally = near_tally + (near_places == picked).astype(jnp.bfloat16)
        late = late_source[:, column].astype(jnp.int16)[None, :]
        hub_tally = hub_tally + (hub_places == late).astype(jnp.bfloat16)
    near_tally = lax.optimization_barrier(near_tally)
    hub_tally = lax.optimization_barrier(hub_tally)
    total = jnp.dot(hidden_one, near_tally, preferred_element_type=jnp.float32)
    total = total + jnp.dot(hub_table, hub_tally, preferred_element_type=jnp.float32)
    mean_two = (total / fanout).astype(jnp.bfloat16)
    own_cols = lax.dynamic_slice_in_dim(own_all, 0, tgt_dev, 1)
    near_cols = lax.dynamic_slice_in_dim(mean_all, 0, tgt_dev, 1)
    own_wide = jnp.maximum(
        left_product(self_one, own_cols) + left_product(neigh_one, near_cols), 0.0
    ).astype(jnp.bfloat16)
    mean_wide = ring_gather(mean_two)
    v_own = lax.dynamic_slice_in_dim(self_two, column_index * hcols, hcols, 1)
    v_near = lax.dynamic_slice_in_dim(neigh_two, column_index * hcols, hcols, 1)
    v_near = jnp.take(v_near.reshape(n_feat, hidden // n_feat, hcols), order, axis=0).reshape(hidden, hcols)
    result = left_product(v_own, own_wide) + left_product(v_near, mean_wide)
    return result.astype(jnp.bfloat16)


def solution(mesh):
    return jax.shard_map(
        body,
        mesh=mesh,
        in_specs=(
            P("feat", "dom"),
            P("dom", None, None),
            P(None, "dom", None),
            P(None, "dom"),
            P("dom", None),
            P("dom", None),
            P(),
            P(),
            P(),
            P(),
        ),
        out_specs=P("feat", "dom"),
        check_vma=False,
    )
```

```python
import math

import jax
import jax.numpy as jnp
from jax import lax
from jax.sharding import PartitionSpec as P


def left_product(weight, columns):
    return lax.dot_general(
        weight, columns, (((0,), (0,)), ((), ())), preferred_element_type=jnp.float32
    )


def pick_columns(data, index, groups=8):
    width, extent = data.shape
    span = extent // groups
    stacked = data.reshape(width, groups, span).transpose(1, 0, 2).reshape(groups * width, span)
    low = (index % span).astype(jnp.int16)
    high = index // span
    places = jnp.arange(span, dtype=jnp.int16)[:, None]
    onehot = (places == low[None, :]).astype(data.dtype)
    rows = jnp.dot(stacked, onehot, preferred_element_type=jnp.float32).astype(data.dtype)
    rows = rows.reshape(groups, width, index.shape[0])
    keep = high[None, None, :] == jnp.arange(groups, dtype=jnp.int32)[:, None, None]
    return jnp.sum(jnp.where(keep, rows, 0), axis=0, dtype=jnp.float32).astype(data.dtype)


def add_columns(values, index, weight, extent, groups=8):
    width, count = values.shape
    span = extent // groups
    values = jnp.concatenate([values, jnp.ones((1, count), values.dtype)], axis=0)
    values = values * weight.astype(values.dtype)[None, :]
    low = (index % span).astype(jnp.int16)
    high = index // span
    keep = high[None, None, :] == jnp.arange(groups, dtype=jnp.int32)[:, None, None]
    spread = jnp.where(keep, values[None], 0).astype(values.dtype).reshape(groups * (width + 1), count)
    places = jnp.arange(span, dtype=jnp.int16)[None, :]
    marks = (low[:, None] == places).astype(values.dtype)
    total = jnp.dot(spread, marks, preferred_element_type=jnp.float32)
    total = total.reshape(groups, width + 1, span).transpose(1, 0, 2).reshape(width + 1, extent)
    return (total[:width], total[width])


def body(
    features,
    edge_source,
    edge_target,
    edge_count,
    hub_local,
    second_source,
    self_one,
    neigh_one,
    self_two,
    neigh_two,
):
    n_feat = lax.axis_size("feat")
    n_dom = lax.axis_size("dom")
    column_index = lax.axis_index("feat")
    narrow, node_dev = features.shape
    sources = edge_source[0]
    slots = sources.shape[1]
    targets = edge_target[:, 0, :]
    counts = edge_count[:, 0]
    live = (jnp.arange(slots, dtype=jnp.int32)[None, :] < counts[:, None]).astype(jnp.float32)
    chosen = pick_columns(features, sources.reshape(-1)).reshape(narrow, n_dom, slots)
    received = lax.all_to_all(chosen, "dom", split_axis=1, concat_axis=1, tiled=True)
    neighbor_total, degree = add_columns(
        received.reshape(narrow, -1), targets.reshape(-1), live.reshape(-1), node_dev
    )
    mean_one = (neighbor_total / jnp.maximum(degree, 1.0)[None, :]).astype(jnp.bfloat16)
    late_source, mean_one = lax.optimization_barrier((second_source, mean_one))
    hidden = self_one.shape[1]
    hcols = hidden // n_feat
    order = (column_index - jnp.arange(n_feat)) % n_feat

    def ring_gather(x):
        parts = [x]
        for shift in range(1, n_feat):
            pairs = [(j, (j + shift) % n_feat) for j in range(n_feat)]
            parts.append(lax.ppermute(x, "feat", perm=pairs))
        return jnp.concatenate(parts, axis=0)

    def ring_rows(weight):
        blocks = weight.reshape(n_feat, narrow, weight.shape[1])
        return jnp.take(blocks, order, axis=0).reshape(n_feat * narrow, weight.shape[1])

    self_one = ring_rows(self_one)
    neigh_one = ring_rows(neigh_one)
    own_all = ring_gather(features)
    mean_all = ring_gather(mean_one)
    w_own = lax.dynamic_slice_in_dim(self_one, column_index * hcols, hcols, 1)
    w_near = lax.dynamic_slice_in_dim(neigh_one, column_index * hcols, hcols, 1)
    pre_one = left_product(w_own, own_all) + left_product(w_near, mean_all)
    hidden_one = jnp.maximum(pre_one, 0.0).astype(jnp.bfloat16)
    hub_marks = (jnp.arange(node_dev, dtype=jnp.int32)[:, None] == hub_local[0][None, :]).astype(jnp.bfloat16)
    hub_rows = jnp.dot(hidden_one, hub_marks, preferred_element_type=jnp.float32).astype(jnp.bfloat16)
    hub_count = hub_rows.shape[1]
    flat = hub_rows.reshape(1, -1)
    spread = jnp.broadcast_to(flat, (n_dom, flat.shape[1]))
    landed = lax.all_to_all(spread, "dom", split_axis=0, concat_axis=0, tiled=True)
    landed = landed.reshape((n_dom,) + hub_rows.shape)
    hub_table = landed.transpose(1, 0, 2).reshape(hidden_one.shape[0], n_dom * hub_count)
    tgt_dev, fanout = second_source.shape
    near_places = jnp.arange(node_dev, dtype=jnp.int16)[:, None]
    hub_places = (node_dev + jnp.arange(n_dom * hub_count, dtype=jnp.int32)).astype(jnp.int16)[:, None]
    near_tally = jnp.zeros((node_dev, tgt_dev), jnp.bfloat16)
    hub_tally = jnp.zeros((n_dom * hub_count, tgt_dev), jnp.bfloat16)
    for column in range(fanout):
        picked = second_source[:, column].astype(jnp.int16)[None, :]
        near_tally = near_tally + (near_places == picked).astype(jnp.bfloat16)
        late = late_source[:, column].astype(jnp.int16)[None, :]
        hub_tally = hub_tally + (hub_places == late).astype(jnp.bfloat16)
    near_tally = lax.optimization_barrier(near_tally)
    hub_tally = lax.optimization_barrier(hub_tally)
    total = jnp.dot(hidden_one, near_tally, preferred_element_type=jnp.float32)
    total = total + jnp.dot(hub_table, hub_tally, preferred_element_type=jnp.float32)
    mean_two = (total / fanout).astype(jnp.bfloat16)
    own_cols = lax.dynamic_slice_in_dim(own_all, 0, tgt_dev, 1)
    near_cols = lax.dynamic_slice_in_dim(mean_all, 0, tgt_dev, 1)
    own_wide = jnp.maximum(
        left_product(self_one, own_cols) + left_product(neigh_one, near_cols), 0.0
    ).astype(jnp.bfloat16)
    mean_wide = ring_gather(mean_two)
    v_own = lax.dynamic_slice_in_dim(self_two, column_index * hcols, hcols, 1)
    v_near = lax.dynamic_slice_in_dim(neigh_two, column_index * hcols, hcols, 1)
    v_near = jnp.take(v_near.reshape(n_feat, hidden // n_feat, hcols), order, axis=0).reshape(hidden, hcols)
    result = left_product(v_own, own_wide) + left_product(v_near, mean_wide)
    return result.astype(jnp.bfloat16)


def solution(mesh):
    return jax.shard_map(
        body,
        mesh=mesh,
        in_specs=(
            P("feat", "dom"),
            P("dom", None, None),
            P(None, "dom", None),
            P(None, "dom"),
            P("dom", None),
            P("dom", None),
            P(),
            P(),
            P(),
            P(),
        ),
        out_specs=P("feat", "dom"),
        check_vma=False,
    )
```

```python
import math

import jax
import jax.numpy as jnp
from jax import lax
from jax.sharding import PartitionSpec as P


def left_product(weight, columns):
    return lax.dot_general(
        weight, columns, (((0,), (0,)), ((), ())), preferred_element_type=jnp.float32
    )


def pick_columns(data, index, groups=16):
    width, extent = data.shape
    span = extent // groups
    stacked = data.reshape(width, groups, span).transpose(1, 0, 2).reshape(groups * width, span)
    low = (index % span).astype(jnp.int16)
    high = index // span
    places = jnp.arange(span, dtype=jnp.int16)[:, None]
    onehot = (places == low[None, :]).astype(data.dtype)
    rows = jnp.dot(stacked, onehot, preferred_element_type=jnp.float32).astype(data.dtype)
    rows = rows.reshape(groups, width, index.shape[0])
    keep = high[None, None, :] == jnp.arange(groups, dtype=jnp.int32)[:, None, None]
    return jnp.sum(jnp.where(keep, rows, 0), axis=0, dtype=jnp.float32).astype(data.dtype)


def add_columns(values, index, weight, extent, groups=8):
    width, count = values.shape
    span = extent // groups
    values = jnp.concatenate([values, jnp.ones((1, count), values.dtype)], axis=0)
    values = values * weight.astype(values.dtype)[None, :]
    low = (index % span).astype(jnp.int16)
    high = index // span
    keep = high[None, None, :] == jnp.arange(groups, dtype=jnp.int32)[:, None, None]
    spread = jnp.where(keep, values[None], 0).astype(values.dtype).reshape(groups * (width + 1), count)
    places = jnp.arange(span, dtype=jnp.int16)[None, :]
    marks = (low[:, None] == places).astype(values.dtype)
    total = jnp.dot(spread, marks, preferred_element_type=jnp.float32)
    total = total.reshape(groups, width + 1, span).transpose(1, 0, 2).reshape(width + 1, extent)
    return (total[:width], total[width])


def body(
    features,
    edge_source,
    edge_target,
    edge_count,
    hub_local,
    second_source,
    self_one,
    neigh_one,
    self_two,
    neigh_two,
):
    n_feat = lax.axis_size("feat")
    n_dom = lax.axis_size("dom")
    column_index = lax.axis_index("feat")
    narrow, node_dev = features.shape
    sources = edge_source[0]
    slots = sources.shape[1]
    targets = edge_target[:, 0, :]
    counts = edge_count[:, 0]
    live = (jnp.arange(slots, dtype=jnp.int32)[None, :] < counts[:, None]).astype(jnp.float32)
    chosen = pick_columns(features, sources.reshape(-1)).reshape(narrow, n_dom, slots)
    received = lax.all_to_all(chosen, "dom", split_axis=1, concat_axis=1, tiled=True)
    neighbor_total, degree = add_columns(
        received.reshape(narrow, -1), targets.reshape(-1), live.reshape(-1), node_dev
    )
    mean_one = (neighbor_total / jnp.maximum(degree, 1.0)[None, :]).astype(jnp.bfloat16)
    late_source, mean_one = lax.optimization_barrier((second_source, mean_one))
    hidden = self_one.shape[1]
    hcols = hidden // n_feat
    order = (column_index - jnp.arange(n_feat)) % n_feat

    def ring_gather(x):
        parts = [x]
        for shift in range(1, n_feat):
            pairs = [(j, (j + shift) % n_feat) for j in range(n_feat)]
            parts.append(lax.ppermute(x, "feat", perm=pairs))
        return jnp.concatenate(parts, axis=0)

    def ring_rows(weight):
        blocks = weight.reshape(n_feat, narrow, weight.shape[1])
        return jnp.take(blocks, order, axis=0).reshape(n_feat * narrow, weight.shape[1])

    self_one = ring_rows(self_one)
    neigh_one = ring_rows(neigh_one)
    own_all = ring_gather(features)
    mean_all = ring_gather(mean_one)
    w_own = lax.dynamic_slice_in_dim(self_one, column_index * hcols, hcols, 1)
    w_near = lax.dynamic_slice_in_dim(neigh_one, column_index * hcols, hcols, 1)
    pre_one = left_product(w_own, own_all) + left_product(w_near, mean_all)
    hidden_one = jnp.maximum(pre_one, 0.0).astype(jnp.bfloat16)
    hub_marks = (jnp.arange(node_dev, dtype=jnp.int32)[:, None] == hub_local[0][None, :]).astype(jnp.bfloat16)
    hub_rows = jnp.dot(hidden_one, hub_marks, preferred_element_type=jnp.float32).astype(jnp.bfloat16)
    hub_count = hub_rows.shape[1]
    spread = jnp.broadcast_to(hub_rows[None], (n_dom,) + hub_rows.shape)
    landed = lax.all_to_all(spread, "dom", split_axis=0, concat_axis=0, tiled=True)
    hub_table = landed.transpose(1, 0, 2).reshape(hidden_one.shape[0], n_dom * hub_count)
    tgt_dev, fanout = second_source.shape
    near_places = jnp.arange(node_dev, dtype=jnp.int16)[:, None]
    hub_places = (node_dev + jnp.arange(n_dom * hub_count, dtype=jnp.int32)).astype(jnp.int16)[:, None]
    near_tally = jnp.zeros((node_dev, tgt_dev), jnp.bfloat16)
    hub_tally = jnp.zeros((n_dom * hub_count, tgt_dev), jnp.bfloat16)
    for column in range(fanout):
        picked = second_source[:, column].astype(jnp.int16)[None, :]
        near_tally = near_tally + (near_places == picked).astype(jnp.bfloat16)
        late = late_source[:, column].astype(jnp.int16)[None, :]
        hub_tally = hub_tally + (hub_places == late).astype(jnp.bfloat16)
    near_tally = lax.optimization_barrier(near_tally)
    hub_tally = lax.optimization_barrier(hub_tally)
    total = jnp.dot(hidden_one, near_tally, preferred_element_type=jnp.float32)
    total = total + jnp.dot(hub_table, hub_tally, preferred_element_type=jnp.float32)
    mean_two = (total / fanout).astype(jnp.bfloat16)
    own_cols = lax.dynamic_slice_in_dim(own_all, 0, tgt_dev, 1)
    near_cols = lax.dynamic_slice_in_dim(mean_all, 0, tgt_dev, 1)
    own_wide = jnp.maximum(
        left_product(self_one, own_cols) + left_product(neigh_one, near_cols), 0.0
    ).astype(jnp.bfloat16)
    mean_wide = ring_gather(mean_two)
    v_own = lax.dynamic_slice_in_dim(self_two, column_index * hcols, hcols, 1)
    v_near = lax.dynamic_slice_in_dim(neigh_two, column_index * hcols, hcols, 1)
    v_near = jnp.take(v_near.reshape(n_feat, hidden // n_feat, hcols), order, axis=0).reshape(hidden, hcols)
    result = left_product(v_own, own_wide) + left_product(v_near, mean_wide)
    return result.astype(jnp.bfloat16)


def solution(mesh):
    return jax.shard_map(
        body,
        mesh=mesh,
        in_specs=(
            P("feat", "dom"),
            P("dom", None, None),
            P(None, "dom", None),
            P(None, "dom"),
            P("dom", None),
            P("dom", None),
            P(),
            P(),
            P(),
            P(),
        ),
        out_specs=P("feat", "dom"),
        check_vma=False,
    )
```

```python
import math

import jax
import jax.numpy as jnp
from jax import lax
from jax.sharding import PartitionSpec as P


def left_product(weight, columns):
    return lax.dot_general(
        weight, columns, (((0,), (0,)), ((), ())), preferred_element_type=jnp.float32
    )


def pick_columns(data, index, groups=4):
    width, extent = data.shape
    span = extent // groups
    stacked = data.reshape(width, groups, span).transpose(1, 0, 2).reshape(groups * width, span)
    low = (index % span).astype(jnp.int16)
    high = index // span
    places = jnp.arange(span, dtype=jnp.int16)[:, None]
    onehot = (places == low[None, :]).astype(data.dtype)
    rows = jnp.dot(stacked, onehot, preferred_element_type=jnp.float32).astype(data.dtype)
    rows = rows.reshape(groups, width, index.shape[0])
    keep = high[None, None, :] == jnp.arange(groups, dtype=jnp.int32)[:, None, None]
    return jnp.sum(jnp.where(keep, rows, 0), axis=0, dtype=jnp.float32).astype(data.dtype)


def add_columns(values, index, weight, extent, groups=8):
    width, count = values.shape
    span = extent // groups
    values = jnp.concatenate([values, jnp.ones((1, count), values.dtype)], axis=0)
    values = values * weight.astype(values.dtype)[None, :]
    low = (index % span).astype(jnp.int16)
    high = index // span
    keep = high[None, None, :] == jnp.arange(groups, dtype=jnp.int32)[:, None, None]
    spread = jnp.where(keep, values[None], 0).astype(values.dtype).reshape(groups * (width + 1), count)
    places = jnp.arange(span, dtype=jnp.int16)[None, :]
    marks = (low[:, None] == places).astype(values.dtype)
    total = jnp.dot(spread, marks, preferred_element_type=jnp.float32)
    total = total.reshape(groups, width + 1, span).transpose(1, 0, 2).reshape(width + 1, extent)
    return (total[:width], total[width])


def body(
    features,
    edge_source,
    edge_target,
    edge_count,
    hub_local,
    second_source,
    self_one,
    neigh_one,
    self_two,
    neigh_two,
):
    n_feat = lax.axis_size("feat")
    n_dom = lax.axis_size("dom")
    column_index = lax.axis_index("feat")
    narrow, node_dev = features.shape
    sources = edge_source[0]
    slots = sources.shape[1]
    targets = edge_target[:, 0, :]
    counts = edge_count[:, 0]
    live = (jnp.arange(slots, dtype=jnp.int32)[None, :] < counts[:, None]).astype(jnp.float32)
    chosen = pick_columns(features, sources.reshape(-1)).reshape(narrow, n_dom, slots)
    received = lax.all_to_all(chosen, "dom", split_axis=1, concat_axis=1, tiled=True)
    neighbor_total, degree = add_columns(
        received.reshape(narrow, -1), targets.reshape(-1), live.reshape(-1), node_dev
    )
    mean_one = (neighbor_total / jnp.maximum(degree, 1.0)[None, :]).astype(jnp.bfloat16)
    late_source, mean_one = lax.optimization_barrier((second_source, mean_one))
    hidden = self_one.shape[1]
    hcols = hidden // n_feat
    order = (column_index - jnp.arange(n_feat)) % n_feat

    def ring_gather(x):
        parts = [x]
        for shift in range(1, n_feat):
            pairs = [(j, (j + shift) % n_feat) for j in range(n_feat)]
            parts.append(lax.ppermute(x, "feat", perm=pairs))
        return jnp.concatenate(parts, axis=0)

    def ring_rows(weight):
        blocks = weight.reshape(n_feat, narrow, weight.shape[1])
        return jnp.take(blocks, order, axis=0).reshape(n_feat * narrow, weight.shape[1])

    self_one = ring_rows(self_one)
    neigh_one = ring_rows(neigh_one)
    own_all = ring_gather(features)
    mean_all = ring_gather(mean_one)
    w_own = lax.dynamic_slice_in_dim(self_one, column_index * hcols, hcols, 1)
    w_near = lax.dynamic_slice_in_dim(neigh_one, column_index * hcols, hcols, 1)
    pre_one = left_product(w_own, own_all) + left_product(w_near, mean_all)
    hidden_one = jnp.maximum(pre_one, 0.0).astype(jnp.bfloat16)
    hub_marks = (jnp.arange(node_dev, dtype=jnp.int32)[:, None] == hub_local[0][None, :]).astype(jnp.bfloat16)
    hub_rows = jnp.dot(hidden_one, hub_marks, preferred_element_type=jnp.float32).astype(jnp.bfloat16)
    hub_count = hub_rows.shape[1]
    spread = jnp.broadcast_to(hub_rows[None], (n_dom,) + hub_rows.shape)
    landed = lax.all_to_all(spread, "dom", split_axis=0, concat_axis=0, tiled=True)
    hub_table = landed.transpose(1, 0, 2).reshape(hidden_one.shape[0], n_dom * hub_count)
    tgt_dev, fanout = second_source.shape
    near_places = jnp.arange(node_dev, dtype=jnp.int16)[:, None]
    hub_places = (node_dev + jnp.arange(n_dom * hub_count, dtype=jnp.int32)).astype(jnp.int16)[:, None]
    near_tally = jnp.zeros((node_dev, tgt_dev), jnp.bfloat16)
    hub_tally = jnp.zeros((n_dom * hub_count, tgt_dev), jnp.bfloat16)
    for column in range(fanout):
        picked = second_source[:, column].astype(jnp.int16)[None, :]
        near_tally = near_tally + (near_places == picked).astype(jnp.bfloat16)
        late = late_source[:, column].astype(jnp.int16)[None, :]
        hub_tally = hub_tally + (hub_places == late).astype(jnp.bfloat16)
    near_tally = lax.optimization_barrier(near_tally)
    hub_tally = lax.optimization_barrier(hub_tally)
    total = jnp.dot(hidden_one, near_tally, preferred_element_type=jnp.float32)
    total = total + jnp.dot(hub_table, hub_tally, preferred_element_type=jnp.float32)
    mean_two = (total / fanout).astype(jnp.bfloat16)
    own_cols = lax.dynamic_slice_in_dim(own_all, 0, tgt_dev, 1)
    near_cols = lax.dynamic_slice_in_dim(mean_all, 0, tgt_dev, 1)
    own_wide = jnp.maximum(
        left_product(self_one, own_cols) + left_product(neigh_one, near_cols), 0.0
    ).astype(jnp.bfloat16)
    mean_wide = ring_gather(mean_two)
    v_own = lax.dynamic_slice_in_dim(self_two, column_index * hcols, hcols, 1)
    v_near = lax.dynamic_slice_in_dim(neigh_two, column_index * hcols, hcols, 1)
    v_near = jnp.take(v_near.reshape(n_feat, hidden // n_feat, hcols), order, axis=0).reshape(hidden, hcols)
    result = left_product(v_own, own_wide) + left_product(v_near, mean_wide)
    return result.astype(jnp.bfloat16)


def solution(mesh):
    return jax.shard_map(
        body,
        mesh=mesh,
        in_specs=(
            P("feat", "dom"),
            P("dom", None, None),
            P(None, "dom", None),
            P(None, "dom"),
            P("dom", None),
            P("dom", None),
            P(),
            P(),
            P(),
            P(),
        ),
        out_specs=P("feat", "dom"),
        check_vma=False,
    )
```
